256 devices in a mesh: facet: 64 (over z, x_lo, y), col: 4 (over x_hi, core).
Axes of the slice: x: 4 (x_hi: 2, x_lo: 2; x = x_hi * 2 + x_lo), y: 4, z: 8, core: 2. Of those that a mesh axis runs over, the one named last changes fastest.
Arguments:
- prepared: bfloat16 [64, 2, 8192, 512], P('facet', None, None, 'col'), may hold values from -6 to 6
- sub_off: int32 [64, 4], P(None, 'col'), may hold values from 0 to 8191
- fac_off: int32 [64], replicated, may hold values from 0 to 511
- win_col: int32 [4, 128], replicated, may hold values from 0 to 255
- vis_weights: bfloat16 [64, 2, 512, 512], P('facet', None, None, 'col'), may hold values from -6 to 6
Outputs:
- facet_strips: bfloat16 [64, 2, 8192, 256], P('facet', None, 'col')
The draws below stay inside these ranges and needn't reach their ends.
All inputs are finite; a program needn't handle non-finite values.
Results may differ from the reference program's by a relative error of at most 0.0093.
Values may be sent and summed in bfloat16 or wider, within the bound.
No kernel may reach another device: no remote copies, remote signals or barrier semaphores. Data moves between devices by JAX's collectives and lax.ppermute only.
A program may use at most 128 MiB of HBM per device.

```python
import math
import jax
import jax.numpy as jnp
from jax import lax

YF = 8192
XM = 128
XA = 512
CW = 128
FACETS = 64
NSUB = 64
OC = 256
N_COL = 4


def touch_ends(drawn, key, smallest, top_value):
    spot = [jax.random.randint(jax.random.fold_in(key, axis), (), 0, length) for axis, length in enumerate(drawn.shape)]
    main_axis = drawn.shape.index(max(drawn.shape))
    neighbour = spot[:main_axis] + [(spot[main_axis] + 1) % drawn.shape[main_axis]] + spot[main_axis + 1:]
    return drawn.at[tuple(spot)].set(smallest).at[tuple(neighbour)].set(top_value)


def levels(key, extent, pieces, smallest, high):
    loudness = 1.0
    for dim, blocks in pieces:
        steps = jax.random.uniform(jax.random.fold_in(jax.random.fold_in(key, 6), dim), (blocks,), jnp.float32, smallest / len(pieces), high / len(pieces))
        loudness = loudness * jnp.repeat(jnp.exp(steps), extent[dim] // blocks).reshape((-1,) + (1,) * (len(extent) - 1 - dim))
    return loudness


def centred(rng, dims, spread, reach, shards=(), held_as=jnp.bfloat16):
    values = jax.random.normal(rng, dims, jnp.float32) * spread
    if len(shards) > 0:
        values = levels(rng, dims, shards, -0.22, 0.18) * values
    return jnp.clip(values, min=-reach, max=reach).astype(held_as)


def setup_inputs(seed: int = 0) -> dict:
    splits = jax.random.split(jax.random.key(seed), 6)
    prepared = centred(splits[0], (FACETS, 2, YF, CW * N_COL), 1.0, 6.0, ((0, 64), (3, 4)))
    sub_off = touch_ends(jax.random.randint(splits[1], (NSUB, N_COL), 0, YF), jax.random.fold_in(splits[1], 1), 0, YF - 1).astype(jnp.int32)
    fac_off = touch_ends(jax.random.randint(splits[2], (FACETS,), 0, XA), jax.random.fold_in(splits[2], 1), 0, XA - 1).astype(jnp.int32)
    win_col = touch_ends(jax.random.randint(splits[3], (N_COL, CW), 0, OC), jax.random.fold_in(splits[3], 1), 0, OC - 1).astype(jnp.int32)
    vis_weights = centred(splits[4], (NSUB, 2, XA, CW * N_COL), 1.0, 6.0, ((0, 64), (3, 4)))
    return {"prepared": prepared, "sub_off": sub_off, "fac_off": fac_off, "win_col": win_col, "vis_weights": vis_weights}


def taper_curve(length):
    position = (jnp.arange(length, dtype=jnp.float32) + 0.5) / length
    return 0.3 + 0.7 * jnp.sin(math.pi * position) ** 2

def phases(row_ids, col_ids, length, sign_factor, scaling):
    products = row_ids[:, None] * col_ids[None, :] % length
    angles = 2.0 * math.pi / length * products.astype(jnp.float32)
    return (jnp.cos(angles) * scaling, sign_factor * jnp.sin(angles) * scaling)

def complex_block(real_part, imag_part):
    upper_rows = jnp.concatenate([real_part, -imag_part], axis=1)
    lower_rows = jnp.concatenate([imag_part, real_part], axis=1)
    return jnp.concatenate([upper_rows, lower_rows], axis=0).astype(jnp.bfloat16)

def small_tables(length):
    positions = jnp.arange(length, dtype=jnp.int32)
    taper_vals = taper_curve(length)
    fwd_re, fwd_im = phases(positions, positions, length, -1.0, 1.0 / math.sqrt(length))
    back_re, back_im = phases(positions, positions, length, 1.0, 1.0 / math.sqrt(length))
    forward = complex_block(fwd_re * taper_vals[None, :], fwd_im * taper_vals[None, :])
    backward = complex_block(back_re * taper_vals[:, None], back_im * taper_vals[:, None])
    return (forward, backward)

def grid_tables(length, facet_count, contrib_len):
    positions = jnp.arange(length, dtype=jnp.int32)
    fwd_re, fwd_im = phases(positions, positions, length, -1.0, 1.0 / math.sqrt(facet_count * contrib_len))
    back_re, back_im = phases(positions, positions, length, 1.0, 1.0 / math.sqrt(length))
    return (complex_block(fwd_re, fwd_im), complex_block(back_re, back_im))

def finish_map(columns, out_cols):
    frequency = jnp.arange(out_cols, dtype=jnp.int32)
    products = columns[:, None] * frequency[None, :] % out_cols
    angles = 2.0 * math.pi / out_cols * products.astype(jnp.float32)
    scaling = 1.0 / math.sqrt(2 * out_cols)
    real_part = jnp.cos(angles) * scaling
    imag_part = jnp.sin(angles) * scaling
    from_real = jnp.concatenate([real_part, imag_part], axis=1)
    from_imag = jnp.concatenate([-imag_part, real_part], axis=1)
    return jnp.stack([from_real, from_imag], axis=0).astype(jnp.bfloat16)

def apply_weights(spectrum, weights):
    spec_re = spectrum[..., 0, :, :]
    spec_im = spectrum[..., 1, :, :]
    weight_re = weights[..., 0, :, :].astype(jnp.float32)
    weight_im = weights[..., 1, :, :].astype(jnp.float32)
    joined = jnp.stack([weight_re * spec_re - weight_im * spec_im, weight_re * spec_im + weight_im * spec_re], axis=-3)
    return joined.astype(jnp.bfloat16)

def reference(prepared, sub_off, fac_off, win_col, vis_weights):
    forward_small, backward_small = small_tables(XM)
    forward_grid, backward_grid = grid_tables(XA, FACETS, XM)
    window_pos = jnp.arange(XM, dtype=jnp.int32)
    dest_rows = ((fac_off[:, None] + window_pos[None, :]) % XA).reshape(-1)

    def one_column(column):
        strips = lax.dynamic_slice_in_dim(prepared, column * CW, CW, 3)
        offsets = lax.dynamic_index_in_dim(sub_off, column, 1, keepdims=False)
        weights = lax.dynamic_slice_in_dim(vis_weights, column * CW, CW, 3)

        def one_subgrid(subgrid_item):
            first_row, weight_block = subgrid_item
            src_rows = (first_row + window_pos) % YF
            picked = strips[:, :, src_rows].reshape(FACETS, 2 * XM, CW)
            contrib = jnp.einsum('ab,fbc->fac', forward_small.astype(jnp.float32), picked.astype(jnp.float32)).astype(jnp.bfloat16)
            flat_rows = contrib.reshape(FACETS, 2, XM, CW).transpose(1, 0, 2, 3).reshape(2, FACETS * XM, CW).astype(jnp.float32)
            assembled = jnp.zeros((2, XA, CW), jnp.float32).at[:, dest_rows].add(flat_rows).astype(jnp.bfloat16)
            spectrum = jnp.dot(forward_grid, assembled.reshape(2 * XA, CW), preferred_element_type=jnp.float32).reshape(2, XA, CW)
            weighted = apply_weights(spectrum, weight_block)
            grid_image = jnp.dot(backward_grid, weighted.reshape(2 * XA, CW), preferred_element_type=jnp.float32).astype(jnp.bfloat16).reshape(2, XA, CW)
            return grid_image[:, dest_rows].reshape(2, FACETS, XM, CW).transpose(1, 0, 2, 3)
        return lax.map(one_subgrid, (offsets, weights))
    returned = lax.map(one_column, jnp.arange(N_COL, dtype=jnp.int32))
    all_rows = (sub_off[:, :, None] + window_pos[None, None, :]) % YF

    def one_facet(facet_index):
        summed = jnp.zeros((YF, 2 * OC), jnp.float32)
        for column in range(N_COL):
            back_part = returned[column, :, facet_index].reshape(NSUB, 2 * XM, CW)
            returned_terms = jnp.einsum('ab,sbc->sac', backward_small.astype(jnp.float32), back_part.astype(jnp.float32))
            returned_terms = returned_terms.reshape(NSUB, 2, XM, CW).transpose(1, 0, 2, 3).reshape(2, NSUB * XM, CW)
            accum = jnp.zeros((2, YF, CW), jnp.float32).at[:, all_rows[:, column].reshape(-1)].add(returned_terms)
            strip_sum = accum.astype(jnp.bfloat16)
            summed = summed + jnp.einsum('pyk,pkm->ym', strip_sum.astype(jnp.float32), finish_map(win_col[column], OC).astype(jnp.float32))
        return summed.astype(jnp.bfloat16).reshape(YF, 2, OC).transpose(1, 0, 2)
    return lax.map(one_facet, jnp.arange(FACETS, dtype=jnp.int32))
```

```python
import math

import jax
import jax.numpy as jnp
import ml_dtypes
import numpy as np
from jax import lax
from jax.experimental import pallas as pl
from jax.experimental.pallas import tpu as pltpu
from jax.sharding import Mesh
from jax.sharding import PartitionSpec as P

XM = 128
LANES = 128
HALF = LANES // 2
BF16 = jnp.bfloat16
F32 = jnp.float32
FACET = ("z", "xl", "y")
NEAR = ("xl", "y")


def side_by_side(real_part, imag_part):
    return np.concatenate([real_part, imag_part], axis=1).astype(ml_dtypes.bfloat16)


def waves(length, sign_factor, scaling):
    positions = np.arange(length)
    angles = 2.0 * np.pi / length * ((positions[:, None] * positions[None, :]) % length)
    return np.cos(angles) * scaling, sign_factor * np.sin(angles) * scaling


def small_tables():
    taper = 0.3 + 0.7 * np.sin(np.pi * (np.arange(XM) + 0.5) / XM) ** 2
    fwd_re, fwd_im = waves(XM, -1.0, 1.0 / math.sqrt(XM))
    back_re, back_im = waves(XM, 1.0, 1.0 / math.sqrt(XM))
    forward = side_by_side(fwd_re * taper[None, :], fwd_im * taper[None, :])
    backward = side_by_side(back_re * taper[:, None], back_im * taper[:, None])
    return forward, backward


def grid_table(grid_len, facet_count):
    coarse = np.arange(0, grid_len, 16)[:, None] * np.arange(grid_len)[None, :] % grid_len
    fine = np.arange(16)[:, None] * np.arange(grid_len)[None, :] % grid_len
    scaling = 1.0 / math.sqrt(facet_count * XM)
    coarse = np.exp(-2j * np.pi * coarse / grid_len) * scaling
    fine = np.exp(-2j * np.pi * fine / grid_len)
    parts = [p.astype(np.float32) for p in (coarse.real, coarse.imag, fine.real, fine.imag)]
    c_re, c_im, f_re, f_im = lax.optimization_barrier(tuple(jnp.asarray(p) for p in parts))
    c_re, c_im = c_re[:, None, :], c_im[:, None, :]
    f_re, f_im = f_re[None, :, :], f_im[None, :, :]
    real_part = (c_re * f_re - c_im * f_im).reshape(grid_len, grid_len).astype(BF16)
    imag_part = (c_re * f_im + c_im * f_re).reshape(grid_len, grid_len).astype(BF16)
    return jnp.concatenate([real_part, imag_part], axis=1)


def finish_maps(columns, out_cols):
    frequency = jnp.arange(out_cols, dtype=jnp.int32)
    products = columns[:, :, None] * frequency[None, None, :] % out_cols
    angles = 2.0 * math.pi / out_cols * products.astype(F32)
    scaling = 1.0 / math.sqrt(2 * out_cols)
    real_part = jnp.cos(angles) * scaling
    imag_part = jnp.sin(angles) * scaling
    from_real = jnp.concatenate([real_part, imag_part], axis=2).astype(BF16)
    from_imag = jnp.concatenate([-imag_part, real_part], axis=2).astype(BF16)
    cols = columns.shape[0]
    shape = (cols, LANES // HALF, 1, HALF, 2 * out_cols)
    both = jnp.concatenate([from_real.reshape(shape), from_imag.reshape(shape)], axis=2)
    return both.transpose(1, 0, 2, 3, 4).reshape(LANES // HALF, cols, LANES, 2 * out_cols)


def low_half(shape):
    return lax.broadcasted_iota(jnp.int32, shape, len(shape) - 1) < HALF


def turn(block):
    swapped = pltpu.roll(block, HALF, 1)
    return jnp.where(low_half(block.shape), -swapped, swapped)


def pack(chunk, real_part, imag_part):
    if chunk == 0:
        return jnp.where(low_half(real_part.shape), real_part, pltpu.roll(imag_part, HALF, 1))
    return jnp.where(low_half(real_part.shape), pltpu.roll(real_part, HALF, 1), imag_part)


def stack_turned(blocks):
    tops = jnp.concatenate(blocks, axis=1)
    lows = jnp.concatenate([turn(b) for b in blocks], axis=1)
    return jnp.concatenate([tops, lows], axis=0).astype(BF16)


def contrib_kernel(chunk, place, starts, strip, table, out, held, source, made_rows, in_sems, out_sems):
    facet_len = strip.shape[1]
    parts = in_sems.shape[0]
    share = facet_len // parts
    tile = 256

    def fetch(p):
        rows = pl.ds(p * share, share)
        return pltpu.make_async_copy(strip.at[:, rows, :], held.at[:, rows, :], in_sems.at[p])

    for p in range(parts):
        fetch(p).start()

    def fill(i, _):
        rows = pl.ds(pl.multiple_of(i * tile, tile), tile)
        source[rows, :] = pack(chunk, held[0, rows, :].astype(F32), held[1, rows, :].astype(F32))
        return 0

    for p in range(parts):
        fetch(p).wait()
        lax.fori_loop(p * (share // tile), (p + 1) * (share // tile), fill, 0)
    source[pl.ds(facet_len, XM), :] = source[pl.ds(0, XM), :]
    planes, depth = out.shape[0], out.shape[1]

    def send(k):
        return pltpu.make_async_copy(made_rows.at[:, k], out.at[:, k], out_sems.at[k])

    def one_group(k, _):
        item = lax.rem(place[0] + k, depth) * planes
        for j in range(0, planes, 2):
            first = source[pl.ds(starts[item + j], XM), :]
            second = source[pl.ds(starts[item + j + 1], XM), :]
            made = jnp.dot(table[...], stack_turned([first, second]), preferred_element_type=F32)
            made_rows[j, k] = made[:, :LANES].astype(BF16)
            made_rows[j + 1, k] = made[:, LANES:].astype(BF16)
        send(k).start()
        return 0

    lax.fori_loop(0, depth, one_group, 0)
    for k in range(depth):
        send(k).wait()


def gather_kernel(chunk, place, offsets, arrived, *refs):
    *outs, held, total, sems = refs
    planes = arrived.shape[0]
    grid_len = total.shape[0] - XM
    base = chunk * grid_len

    def fetch(k):
        return pltpu.make_async_copy(arrived.at[:, k], held.at[:, k], sems.at[k])

    for k in range(len(outs)):
        fetch(k).start()
    for k, out in enumerate(outs):
        total[...] = jnp.zeros_like(total)
        fetch(k).wait()

        def one_facet(j, _, k=k):
            rows = pl.ds(offsets[place[0] * planes + j], XM)
            total[rows, :] = total[rows, :] + held[j, k].astype(F32)
            return 0

        lax.fori_loop(0, planes, one_facet, 0, unroll=2)
        total[pl.ds(0, XM), :] = total[pl.ds(0, XM), :] + total[pl.ds(grid_len, XM), :]
        out[pl.ds(base, grid_len), :] = total[pl.ds(0, grid_len), :].astype(BF16)
        if base > 0:
            out[pl.ds(0, base), :] = jnp.zeros((base, LANES), BF16)


def grid_kernel(chunk, weights, table, *refs):
    *parts, out = refs
    grid_len = weights.shape[1]
    rows = pl.ds(chunk * grid_len, grid_len)
    total = parts[0][rows, :].astype(F32)
    for part in parts[1:]:
        total = total + part[rows, :].astype(F32)
    assembled = total.astype(BF16).astype(F32)
    spectrum = jnp.dot(table[...], stack_turned([assembled]), preferred_element_type=F32)
    weight_re = weights[0].astype(F32)
    weight_im = weights[1].astype(F32)
    both_re = pack(chunk, weight_re, weight_re)
    both_im = pack(chunk, weight_im, weight_im)
    weighted = (both_re * spectrum + both_im * turn(spectrum)).astype(BF16).astype(F32)
    back = jnp.concatenate([weighted, -turn(weighted)], axis=0).astype(BF16)
    image = jnp.dot(table[...], back, preferred_element_type=F32)
    out[pl.ds(0, grid_len), :] = (image * 4.0).astype(BF16)
    if chunk == 0:
        out[pl.ds(grid_len, grid_len), :] = jnp.zeros((grid_len, LANES), BF16)


def spread_kernel(place, offsets, *refs):
    *images, out, wide, made_rows, sems = refs
    grid_len = wide.shape[0] - XM
    planes = out.shape[0]

    def send(k):
        return pltpu.make_async_copy(made_rows.at[:, k], out.at[:, k], sems.at[k])

    for k, image in enumerate(images):
        wide[pl.ds(0, grid_len), :] = image[pl.ds(0, grid_len), :].astype(F32)
        wide[pl.ds(grid_len, XM), :] = wide[pl.ds(0, XM), :]

        def one_facet(j, _, k=k):
            rows = pl.ds(offsets[place[0] * planes + j], XM)
            made_rows[j, k] = wide[rows, :].astype(BF16)
            return 0

        lax.fori_loop(0, planes, one_facet, 0, unroll=2)
        send(k).start()
    for k in range(len(images)):
        send(k).wait()


def accum_kernel(place, starts, returned, table, *refs):
    *outs, held, total, sems = refs
    planes, depth = returned.shape[0], returned.shape[1]
    own_rows = outs[0].shape[0]
    facet_len = own_rows * len(outs)

    def fetch(k):
        return pltpu.make_async_copy(returned.at[:, k], held.at[:, k], sems.at[k])

    for k in range(depth):
        fetch(k).start()
    total[...] = jnp.zeros_like(total)

    def one_group(k, _):
        fetch(k).wait()
        item = lax.rem(place[0] + depth - k, depth) * planes
        for j in range(0, planes, 2):
            blocks = [held[j, k].astype(F32), held[j + 1, k].astype(F32)]
            made = jnp.dot(table[...], stack_turned(blocks), preferred_element_type=F32)
            for n in range(2):
                rows = pl.ds(starts[item + j + n], XM)
                total[rows, :] = total[rows, :] + made[:, n * LANES : (n + 1) * LANES]
        return 0

    lax.fori_loop(0, depth, one_group, 0)
    total[pl.ds(0, XM), :] = total[pl.ds(0, XM), :] + total[pl.ds(facet_len, XM), :]
    tile = 256
    for k, out in enumerate(outs):
        first = jnp.bitwise_xor(place[1], k) * own_rows

        def drain(i, _, out=out, first=first):
            rows = pl.ds(pl.multiple_of(first + i * tile, tile), tile)
            out[pl.ds(pl.multiple_of(i * tile, tile), tile), :] = total[rows, :].astype(BF16)
            return 0

        lax.fori_loop(0, own_rows // tile, drain, 0)


def window(place, strips, maps):
    made = None
    for k, strip in enumerate(strips):
        term = jnp.dot(
            strip[...], maps[jnp.bitwise_xor(place[1], k)], preferred_element_type=F32
        )
        made = term if made is None else made + term
    return made


def half_kernel(place, maps, *strips_and_out):
    *strips, out = strips_and_out
    out[...] = window(place, strips, maps)


def finish_kernel(place, maps, made, *strips_and_out):
    *strips, out = strips_and_out
    out_cols = out.shape[2]
    both = made[...] + window(place, strips, maps)
    out[0] = both[:, :out_cols].astype(BF16)
    out[1] = both[:, out_cols:].astype(BF16)


SMEM = pl.BlockSpec(memory_space=pltpu.SMEM)
VMEM = pl.BlockSpec(memory_space=pltpu.VMEM)
HBM = pl.BlockSpec(memory_space=pltpu.HBM)


def call(kernel, name, outs, in_specs, scratch, micros, limit, where=VMEM):
    shapes = [jax.ShapeDtypeStruct(s, BF16) for s in outs]
    one = len(outs) == 1
    return pl.pallas_call(
        kernel,
        name=name,
        out_shape=shapes[0] if one else shapes,
        in_specs=in_specs,
        out_specs=where if one else [where] * len(outs),
        scratch_shapes=scratch,
        compiler_params=pltpu.CompilerParams(vmem_limit_bytes=limit << 20),
        cost_estimate=cost(micros),
    )


def cost(micros):
    return pl.CostEstimate(flops=0, bytes_accessed=int(micros * 3.5e6), transcendentals=0)


def bind(kernel, chunk):
    def bound(*refs):
        kernel(chunk, *refs)

    return bound


def shifted(value, step):
    size = lax.axis_size("z")
    return lax.ppermute(value, "z", [(i, (i + step) % size) for i in range(size)])


def swapped(value, flip):
    return lax.ppermute(value, "col", [(i, i ^ flip) for i in range(lax.axis_size("col"))])


def add(first, second):
    return (first.astype(F32) + second.astype(F32)).astype(BF16)


def body(prepared, sub_off, fac_off, win_col, vis_weights):
    depth = lax.axis_size("z")
    planes = lax.axis_size(NEAR)
    facet_count = fac_off.shape[0]
    strip = prepared[0]
    weights = vis_weights[0]
    facet_len = strip.shape[1]
    grid_len = weights.shape[1]
    col_count = lax.axis_size("col")
    own_rows = facet_len // col_count
    out_cols = LANES * col_count // 2
    place = jnp.stack([lax.axis_index("z"), lax.axis_index("col")]).astype(jnp.int32)
    starts = jnp.bitwise_and(sub_off[:, 0], facet_len - 1)
    offsets = jnp.bitwise_and(fac_off, grid_len - 1)
    forward_small, backward_small = small_tables()
    grid_forward = grid_table(grid_len, facet_count)
    blocks = (planes, depth, XM, LANES)
    flips = sorted(range(1, col_count), reverse=True)

    long_rows = pltpu.VMEM((facet_len + XM, LANES), F32)
    grid_rows = pltpu.VMEM((grid_len + XM, LANES), F32)
    all_blocks = pltpu.VMEM(blocks, BF16)
    sems = pltpu.SemaphoreType.DMA((depth,))

    def contrib(c, strip):
        return call(
            bind(contrib_kernel, c), f"contrib{c}", [blocks], [SMEM, SMEM, HBM, VMEM],
            [pltpu.VMEM(strip.shape, BF16), long_rows, all_blocks, pltpu.SemaphoreType.DMA((8,)), sems],
            6.5, 63, HBM,
        )(place, starts, strip, forward_small)

    def near(value):
        return lax.all_to_all(value, NEAR, 0, 0, tiled=True)

    def gather(c, arrived):
        return call(
            bind(gather_kernel, c), f"gather{c}", [(grid_len * (1 + c), LANES)] * depth, [SMEM, SMEM, HBM],
            [all_blocks, grid_rows, sems], 2, 8,
        )(place, offsets, arrived)

    def image_of(c, parts):
        return call(
            bind(grid_kernel, c), f"grid{c}", [(grid_len * (2 - c), LANES)], [VMEM] * (2 + len(parts)), [], 1.5, 12
        )(weights, grid_forward, *parts)

    def spread(c, images):
        return call(
            spread_kernel, f"spread{c}", [blocks], [SMEM, SMEM] + [VMEM] * depth,
            [grid_rows, all_blocks, sems], 2, 8, HBM,
        )(place, offsets, *images)

    def accum(c, returned):
        return call(
            accum_kernel, f"accum{c}", [(own_rows, LANES)] * col_count,
            [SMEM, SMEM, HBM, VMEM], [all_blocks, long_rows, sems], 6, 14,
        )(place, starts, returned, backward_small)

    def exchange(summed):
        moved = {k: swapped(summed[k], k) for k in flips}
        return [summed[0]] + [moved[k] for k in range(1, col_count)]

    far, near_side = depth // 2, (depth - 1) // 2

    def reduce_step(parts, state, i):
        up, down = state
        up = shifted(up, 1)
        if i < far - 1:
            up = add(up, parts[far - 1 - i])
        if i < near_side:
            down = shifted(down, -1)
            if i < near_side - 1:
                down = add(down, parts[far + 2 + i])
        return up, down

    def share_step(state, i):
        up, down = state
        up = up + [shifted(up[-1], 1)]
        if i < near_side:
            down = down + [shifted(down[-1], -1)]
        return up, down

    def shared(state):
        up, down = state
        return up + down[:0:-1]

    barrier = lax.optimization_barrier
    maps = finish_maps(win_col, out_cols)
    payload0 = contrib(0, strip)
    payload0, strip = barrier((payload0, strip))
    arrived0 = near(payload0)
    payload1 = contrib(1, strip)
    arrived0, payload1, maps, grid_forward = barrier((arrived0, payload1, maps, grid_forward))
    arrived1 = near(payload1)
    parts0 = gather(0, arrived0)
    reduced0 = parts0[far], parts0[far + 1]
    for i in range(far):
        reduced0 = reduce_step(parts0, reduced0, i)
    image0 = image_of(0, [parts0[0], *reduced0])
    parts1 = gather(1, arrived1)
    image0, parts1 = barrier((image0, parts1))
    up, down = add(image0, parts1[far]), add(image0, parts1[far + 1])
    ups, downs = [], []
    for i in range(far):
        up = shifted(up, 1)
        ups.append(up)
        if i < near_side:
            down = shifted(down, -1)
            downs.append(down)
        if i < far - 1:
            up = add(up, parts1[far - 1 - i])
        if i < near_side - 1:
            down = add(down, parts1[far + 2 + i])
    image1 = image_of(1, [parts1[0], up, down])
    images0 = [image0] + ups + downs[::-1]
    image1, images0 = barrier((image1, images0))
    returned0 = near(spread(0, images0))
    share1 = [image1], [image1]
    for i in range(far):
        share1 = share_step(share1, i)
    spread1 = spread(1, shared(share1))
    returned0, spread1 = barrier((returned0, spread1))
    returned1 = near(spread1)
    strips0 = exchange(accum(0, returned0))
    strips1 = exchange(accum(1, returned1))

    tile = min(512, own_rows)
    strip_spec = pl.BlockSpec((tile, LANES), lambda i: (i, 0))
    maps_spec = pl.BlockSpec(maps.shape[1:], lambda i: (0, 0, 0))
    wide_spec = pl.BlockSpec((tile, 2 * out_cols), lambda i: (i, 0))
    half = pl.pallas_call(
        half_kernel,
        name="half",
        grid=(own_rows // tile,),
        out_shape=jax.ShapeDtypeStruct((own_rows, 2 * out_cols), F32),
        in_specs=[SMEM, maps_spec] + [strip_spec] * col_count,
        out_specs=wide_spec,
        compiler_params=pltpu.CompilerParams(vmem_limit_bytes=16 << 20),
        cost_estimate=cost(4),
    )(place, maps[0], *strips0)
    result = pl.pallas_call(
        finish_kernel,
        name="finish",
        grid=(own_rows // tile,),
        out_shape=jax.ShapeDtypeStruct((2, own_rows, out_cols), BF16),
        in_specs=[SMEM, maps_spec, wide_spec] + [strip_spec] * col_count,
        out_specs=pl.BlockSpec((2, tile, out_cols), lambda i: (0, i, 0)),
        compiler_params=pltpu.CompilerParams(vmem_limit_bytes=16 << 20),
        cost_estimate=cost(4),
    )(place, maps[1], half, *strips1)
    return result[None]


def solution(mesh):
    facets, cols = mesh.devices.shape
    fine = Mesh(
        mesh.devices.reshape(facets // 8, 2, 4, cols), ("z", "xl", "y", "col")
    )
    in_specs = (
        P(FACET, None, None, "col"),
        P(None, "col"),
        P(),
        P(),
        P(FACET, None, None, "col"),
    )
    out_specs = P(FACET, None, "col", None)
    return jax.shard_map(body, mesh=fine, in_specs=in_specs, out_specs=out_specs, check_vma=False)
```

```python
import math

import jax
import jax.numpy as jnp
import ml_dtypes
import numpy as np
from jax import lax
from jax.experimental import pallas as pl
from jax.experimental.pallas import tpu as pltpu
from jax.sharding import Mesh
from jax.sharding import PartitionSpec as P

XM = 128
LANES = 128
HALF = LANES // 2
BF16 = jnp.bfloat16
F32 = jnp.float32
FACET = ("zq", "zp", "xl", "y")
NEAR = (("zp", "xl", "y"), ("xl", "y"))
FAR = (("zq",), ("zq", "zp"))


def side_by_side(real_part, imag_part):
    return np.concatenate([real_part, imag_part], axis=1).astype(ml_dtypes.bfloat16)


def waves(length, sign_factor, scaling):
    positions = np.arange(length)
    angles = 2.0 * np.pi / length * ((positions[:, None] * positions[None, :]) % length)
    return np.cos(angles) * scaling, sign_factor * np.sin(angles) * scaling


def small_tables():
    taper = 0.3 + 0.7 * np.sin(np.pi * (np.arange(XM) + 0.5) / XM) ** 2
    fwd_re, fwd_im = waves(XM, -1.0, 1.0 / math.sqrt(XM))
    back_re, back_im = waves(XM, 1.0, 1.0 / math.sqrt(XM))
    forward = side_by_side(fwd_re * taper[None, :], fwd_im * taper[None, :])
    backward = side_by_side(back_re * taper[:, None], back_im * taper[:, None])
    return forward, backward


def grid_table(grid_len, facet_count):
    coarse = np.arange(0, grid_len, 16)[:, None] * np.arange(grid_len)[None, :] % grid_len
    fine = np.arange(16)[:, None] * np.arange(grid_len)[None, :] % grid_len
    scaling = 1.0 / math.sqrt(facet_count * XM)
    coarse = np.exp(-2j * np.pi * coarse / grid_len) * scaling
    fine = np.exp(-2j * np.pi * fine / grid_len)
    parts = [p.astype(np.float32) for p in (coarse.real, coarse.imag, fine.real, fine.imag)]
    c_re, c_im, f_re, f_im = lax.optimization_barrier(tuple(jnp.asarray(p) for p in parts))
    c_re, c_im = c_re[:, None, :], c_im[:, None, :]
    f_re, f_im = f_re[None, :, :], f_im[None, :, :]
    real_part = (c_re * f_re - c_im * f_im).reshape(grid_len, grid_len).astype(BF16)
    imag_part = (c_re * f_im + c_im * f_re).reshape(grid_len, grid_len).astype(BF16)
    return jnp.concatenate([real_part, imag_part], axis=1)


def finish_maps(columns, out_cols):
    frequency = jnp.arange(out_cols, dtype=jnp.int32)
    products = columns[:, :, None] * frequency[None, None, :] % out_cols
    angles = 2.0 * math.pi / out_cols * products.astype(F32)
    scaling = 1.0 / math.sqrt(2 * out_cols)
    real_part = jnp.cos(angles) * scaling
    imag_part = jnp.sin(angles) * scaling
    from_real = jnp.concatenate([real_part, imag_part], axis=2).astype(BF16)
    from_imag = jnp.concatenate([-imag_part, real_part], axis=2).astype(BF16)
    cols = columns.shape[0]
    shape = (cols, LANES // HALF, 1, HALF, 2 * out_cols)
    both = jnp.concatenate([from_real.reshape(shape), from_imag.reshape(shape)], axis=2)
    return both.transpose(1, 0, 2, 3, 4).reshape(LANES // HALF, cols, LANES, 2 * out_cols)


def low_half(shape):
    return lax.broadcasted_iota(jnp.int32, shape, len(shape) - 1) < HALF


def turn(block):
    swapped = pltpu.roll(block, HALF, 1)
    return jnp.where(low_half(block.shape), -swapped, swapped)


def pack(chunk, real_part, imag_part):
    if chunk == 0:
        return jnp.where(low_half(real_part.shape), real_part, pltpu.roll(imag_part, HALF, 1))
    return jnp.where(low_half(real_part.shape), pltpu.roll(real_part, HALF, 1), imag_part)


def stack_turned(blocks):
    tops = jnp.concatenate(blocks, axis=1)
    lows = jnp.concatenate([turn(b) for b in blocks], axis=1)
    return jnp.concatenate([tops, lows], axis=0).astype(BF16)


def window_rows(first_rows, item, length):
    return pl.ds(jnp.bitwise_and(first_rows[item], length - 1), XM)


def contrib_kernel(chunk, starts, strip, table, out, held, source, made_rows, in_sems, out_sems):
    facet_len = strip.shape[1]
    parts = in_sems.shape[0]
    share = facet_len // parts
    tile = 256

    def fetch(p):
        rows = pl.ds(p * share, share)
        return pltpu.make_async_copy(strip.at[:, rows, :], held.at[:, rows, :], in_sems.at[p])

    for p in range(parts):
        fetch(p).start()

    def fill(i, _):
        rows = pl.ds(pl.multiple_of(i * tile, tile), tile)
        source[rows, :] = pack(chunk, held[0, rows, :].astype(F32), held[1, rows, :].astype(F32))
        return 0

    for p in range(parts):
        fetch(p).wait()
        lax.fori_loop(p * (share // tile), (p + 1) * (share // tile), fill, 0)
    source[pl.ds(facet_len, XM), :] = source[pl.ds(0, XM), :]
    planes, depth = out.shape[0], out.shape[1]

    def send(k):
        return pltpu.make_async_copy(made_rows.at[:, k], out.at[:, k], out_sems.at[k])

    def one_group(k, _):
        for j in range(0, planes, 2):
            first = source[window_rows(starts, k * planes + j, facet_len), :]
            second = source[window_rows(starts, k * planes + j + 1, facet_len), :]
            made = jnp.dot(table[...], stack_turned([first, second]), preferred_element_type=F32)
            made_rows[j, k] = made[:, :LANES].astype(BF16)
            made_rows[j + 1, k] = made[:, LANES:].astype(BF16)
        send(k).start()
        return 0

    lax.fori_loop(0, depth, one_group, 0)
    for k in range(depth):
        send(k).wait()


def gather_kernel(chunk, place, offsets, arrived, *refs):
    *outs, held, total, sems = refs
    planes, depth = arrived.shape[0], arrived.shape[1]
    grid_len = total.shape[0] - XM
    owners = [lax.rem(place[chunk] + k * (1 if chunk == 0 else place[3]), depth) for k in range(depth)]

    def fetch(owner):
        return pltpu.make_async_copy(arrived.at[:, owner], held.at[:, owner], sems.at[owner])

    for owner in owners:
        fetch(owner).start()
    for owner, out in zip(owners, outs):
        total[...] = jnp.zeros_like(total)
        fetch(owner).wait()

        def one_facet(j, _, owner=owner):
            rows = window_rows(offsets, place[chunk] * planes + j, grid_len)
            total[rows, :] = total[rows, :] + held[j, owner].astype(F32)
            return 0

        lax.fori_loop(0, planes, one_facet, 0, unroll=2)
        total[pl.ds(0, XM), :] = total[pl.ds(0, XM), :] + total[pl.ds(grid_len, XM), :]
        base = out.shape[0] - grid_len
        out[pl.ds(base, grid_len), :] = total[pl.ds(0, grid_len), :].astype(BF16)
        if base > 0:
            out[pl.ds(0, base), :] = jnp.zeros((base, LANES), BF16)


def grid_kernel(chunk, weights, table, *refs):
    *parts, out = refs
    grid_len = weights.shape[1]
    total = 0.0
    for part in parts:
        total = total + part[pl.ds(part.shape[0] - grid_len, grid_len), :].astype(F32)
    assembled = total.astype(BF16).astype(F32)
    spectrum = jnp.dot(table[...], stack_turned([assembled]), preferred_element_type=F32)
    weight_re = weights[0].astype(F32)
    weight_im = weights[1].astype(F32)
    both_re = pack(chunk, weight_re, weight_re)
    both_im = pack(chunk, weight_im, weight_im)
    weighted = (both_re * spectrum + both_im * turn(spectrum)).astype(BF16).astype(F32)
    back = jnp.concatenate([weighted, -turn(weighted)], axis=0).astype(BF16)
    image = jnp.dot(table[...], back, preferred_element_type=F32)
    out[...] = (image * 4.0).astype(BF16)


def spread_kernel(place, offsets, *refs):
    *images, out, wide, made_rows, sems = refs
    grid_len = wide.shape[0] - XM
    planes = out.shape[0]

    def send(k):
        return pltpu.make_async_copy(made_rows.at[:, k], out.at[:, k], sems.at[k])

    for k, image in enumerate(images):
        wide[pl.ds(0, grid_len), :] = image[pl.ds(0, grid_len), :].astype(F32)
        wide[pl.ds(grid_len, XM), :] = wide[pl.ds(0, XM), :]

        def one_facet(j, _, k=k):
            rows = window_rows(offsets, place[1] * planes + j, grid_len)
            made_rows[j, k] = wide[rows, :].astype(BF16)
            return 0

        lax.fori_loop(0, planes, one_facet, 0, unroll=2)
        send(k).start()
    for k in range(len(images)):
        send(k).wait()


def accum_kernel(place, starts, returned, table, *refs):
    *outs, held, total, sems = refs
    planes, depth = returned.shape[0], returned.shape[1]
    own_rows = outs[0].shape[0]
    facet_len = own_rows * len(outs)

    def fetch(k):
        return pltpu.make_async_copy(returned.at[:, k], held.at[:, k], sems.at[k])

    for k in range(depth):
        fetch(k).start()
    total[...] = jnp.zeros_like(total)

    def one_group(k, _):
        fetch(k).wait()
        item = lax.rem(place[1] + k * (depth - place[3]), depth) * planes
        for j in range(0, planes, 2):
            blocks = [held[j, k].astype(F32), held[j + 1, k].astype(F32)]
            made = jnp.dot(table[...], stack_turned(blocks), preferred_element_type=F32)
            for n in range(2):
                rows = window_rows(starts, item + j + n, facet_len)
                total[rows, :] = total[rows, :] + made[:, n * LANES : (n + 1) * LANES]
        return 0

    lax.fori_loop(0, depth, one_group, 0)
    total[pl.ds(0, XM), :] = total[pl.ds(0, XM), :] + total[pl.ds(facet_len, XM), :]
    tile = 256
    for k, out in enumerate(outs):
        first = jnp.bitwise_xor(place[2], k) * own_rows

        def drain(i, _, out=out, first=first):
            rows = pl.ds(pl.multiple_of(first + i * tile, tile), tile)
            out[pl.ds(pl.multiple_of(i * tile, tile), tile), :] = total[rows, :].astype(BF16)
            return 0

        lax.fori_loop(0, own_rows // tile, drain, 0)


def window(place, terms, maps):
    made = None
    for chunk, k, strip in terms:
        table = maps[chunk, jnp.bitwise_xor(place[2], k)]
        term = jnp.dot(strip[...], table, preferred_element_type=F32)
        made = term if made is None else made + term
    return made


def half_kernel(keys, place, maps, *strips_and_out):
    *strips, out = strips_and_out
    out[...] = window(place, [(*key, s) for key, s in zip(keys, strips)], maps)


def finish_kernel(keys, place, maps, made, *strips_and_out):
    *strips, out = strips_and_out
    out_cols = out.shape[2]
    both = made[...] + window(place, [(*key, s) for key, s in zip(keys, strips)], maps)
    out[0] = both[:, :out_cols].astype(BF16)
    out[1] = both[:, out_cols:].astype(BF16)


SMEM = pl.BlockSpec(memory_space=pltpu.SMEM)
VMEM = pl.BlockSpec(memory_space=pltpu.VMEM)
HBM = pl.BlockSpec(memory_space=pltpu.HBM)


def call(kernel, name, outs, in_specs, scratch, micros, limit, where=VMEM):
    shapes = [jax.ShapeDtypeStruct(s, BF16) for s in outs]
    one = len(outs) == 1
    return pl.pallas_call(
        kernel,
        name=name,
        out_shape=shapes[0] if one else shapes,
        in_specs=in_specs,
        out_specs=where if one else [where] * len(outs),
        scratch_shapes=scratch,
        compiler_params=pltpu.CompilerParams(vmem_limit_bytes=limit << 20),
        cost_estimate=cost(micros),
    )


def cost(micros):
    return pl.CostEstimate(flops=0, bytes_accessed=int(micros * 3.5e6), transcendentals=0)


def bind(kernel, chunk):
    def bound(*refs):
        kernel(chunk, *refs)

    return bound


def shifted(value, step):
    size = lax.axis_size("zq")
    return lax.ppermute(value, "zq", [(i, (i + step) % size) for i in range(size)])


def turned(value, step):
    size, cols = lax.axis_size(FAR[1]), lax.axis_size("col")
    perm = [
        (i * cols + c, (i + (step if c % 2 == 0 else -step)) % size * cols + c)
        for i in range(size)
        for c in range(cols)
    ]
    return lax.ppermute(value, (*FAR[1], "col"), perm)


def swapped(value, flip):
    return lax.ppermute(value, "col", [(i, i ^ flip) for i in range(lax.axis_size("col"))])


def add(first, second):
    return (first.astype(F32) + second.astype(F32)).astype(BF16)


def body(prepared, sub_off, fac_off, win_col, vis_weights):
    facet_count = fac_off.shape[0]
    strip = prepared[0]
    weights = vis_weights[0]
    facet_len = strip.shape[1]
    grid_len = weights.shape[1]
    col_count = lax.axis_size("col")
    own_rows = facet_len // col_count
    out_cols = LANES * col_count // 2
    place = [lax.axis_index(FAR[0]), lax.axis_index(FAR[1]), lax.axis_index("col")]
    size = lax.axis_size(FAR[1])
    place.append(jnp.where(place[2] % 2 == 0, 1, size - 1))
    place = jnp.stack(place).astype(jnp.int32)
    starts = sub_off.reshape(-1)
    forward_small, backward_small = small_tables()
    grid_forward = grid_table(grid_len, facet_count)
    flips = sorted(range(1, col_count), reverse=True)
    long_rows = pltpu.VMEM((facet_len + XM, LANES), F32)
    grid_rows = pltpu.VMEM((grid_len + XM, LANES), F32)
    planes = [lax.axis_size(axes) for axes in NEAR]
    depths = [lax.axis_size(axes) for axes in FAR]
    blocks = [(p, d, XM, LANES) for p, d in zip(planes, depths)]
    held = [pltpu.VMEM(b, BF16) for b in blocks]
    sems = [pltpu.SemaphoreType.DMA((d,)) for d in depths]

    def contrib(c, strip):
        return call(
            bind(contrib_kernel, c), f"contrib{c}", [blocks[c]], [SMEM, HBM, VMEM],
            [pltpu.VMEM(strip.shape, BF16), long_rows, held[c], pltpu.SemaphoreType.DMA((8,)), sems[c]],
            8, 63, HBM,
        )(starts, strip, forward_small)

    def near(c, value):
        return lax.all_to_all(value, NEAR[c], 0, 0, tiled=True)

    def gather(c, arrived, doubled):
        outs = [(grid_len * (1 + (k in doubled)), LANES) for k in range(depths[c])]
        return call(
            bind(gather_kernel, c), f"gather{c}", outs,
            [SMEM, SMEM, HBM], [held[c], grid_rows, sems[c]], 2, 8,
        )(place, fac_off, arrived)

    def image_of(c, parts):
        return call(
            bind(grid_kernel, c), f"grid{c}", [(grid_len, LANES)], [VMEM] * (2 + len(parts)),
            [], 1.5, 12,
        )(weights, grid_forward, *parts)

    def spread(c, images):
        return call(
            spread_kernel, f"spread{c}", [blocks[1]], [SMEM, SMEM] + [VMEM] * depths[1],
            [grid_rows, held[1], sems[1]], 2, 8, HBM,
        )(place, fac_off, *images)

    def accum(c, returned):
        return call(
            accum_kernel, f"accum{c}", [(own_rows, LANES)] * col_count,
            [SMEM, SMEM, HBM, VMEM], [held[1], long_rows, sems[1]], 5, 14,
        )(place, starts, returned, backward_small)

    def exchange(summed):
        moved = {k: swapped(summed[k], k) for k in flips}
        return [summed[0]] + [moved[k] for k in range(1, col_count)]

    barrier = lax.optimization_barrier
    maps = finish_maps(win_col, out_cols)
    payload0 = contrib(0, strip)
    payload0, strip = barrier((payload0, strip))
    arrived0 = near(0, payload0)
    payload1 = contrib(1, strip)
    arrived0, payload1, maps, grid_forward = barrier((arrived0, payload1, maps, grid_forward))
    arrived1 = near(1, payload1)

    steps = sorted(range(1, depths[0]), key=lambda k: -min(k, depths[0] - k))
    parts0 = gather(0, arrived0, ())
    image0 = image_of(0, [parts0[0]] + [shifted(parts0[k], k) for k in steps])

    far, near_side = depths[1] // 2, (depths[1] - 1) // 2
    doubled = [*range(2, far), *range(far + 2, depths[1] - 1)]
    parts1 = gather(1, arrived1, doubled)
    ups, downs = [turned(image0, 1)], [turned(image0, -1)]
    up = jnp.concatenate([ups[0], parts1[far]])
    down = jnp.concatenate([downs[0], parts1[far + 1]])
    for i in range(far - 1):
        up = turned(up, 1)
        ups.append(up)
        if i < far - 2:
            up = add(up, parts1[far - 1 - i])
    for i in range(near_side - 1):
        down = turned(down, -1)
        downs.append(down)
        if i < near_side - 2:
            down = add(down, parts1[far + 2 + i])
    up = turned(add(up[grid_len:], parts1[1]), 1)
    down = turned(add(down[grid_len:], parts1[depths[1] - 1]), -1)
    images0 = [image0] + ups + downs[::-1]
    image1 = image_of(1, [parts1[0], up, down])
    images0[0], image1 = barrier((image0, image1))
    returned0 = near(1, spread(0, images0))

    ups, downs = [image1], [image1]
    for i in range(far):
        ups.append(turned(ups[-1], 1))
        if i < near_side:
            downs.append(turned(downs[-1], -1))
    spread1 = spread(1, ups + downs[:0:-1])
    returned0, spread1 = barrier((returned0, spread1))
    returned1 = near(1, spread1)
    accum0 = accum(0, returned0)
    strips0 = exchange(accum0)
    strips1 = exchange(accum(1, returned1))

    tile = min(512, own_rows)
    strip_spec = pl.BlockSpec((tile, LANES), lambda i: (i, 0))
    maps_spec = pl.BlockSpec(maps.shape, lambda i: (0, 0, 0, 0))
    wide_spec = pl.BlockSpec((tile, 2 * out_cols), lambda i: (i, 0))
    late = [(1, k) for k in range(2, col_count)]
    early = [(0, k) for k in range(col_count)] + [(1, 0), (1, 1)]
    strips = (strips0, strips1)
    half = pl.pallas_call(
        bind(half_kernel, early),
        name="half",
        grid=(own_rows // tile,),
        out_shape=jax.ShapeDtypeStruct((own_rows, 2 * out_cols), F32),
        in_specs=[SMEM, maps_spec] + [strip_spec] * len(early),
        out_specs=wide_spec,
        compiler_params=pltpu.CompilerParams(vmem_limit_bytes=16 << 20),
        cost_estimate=cost(4),
    )(place, maps, *[strips[c][k] for c, k in early])
    result = pl.pallas_call(
        bind(finish_kernel, late),
        name="finish",
        grid=(own_rows // tile,),
        out_shape=jax.ShapeDtypeStruct((2, own_rows, out_cols), BF16),
        in_specs=[SMEM, maps_spec, wide_spec] + [strip_spec] * len(late),
        out_specs=pl.BlockSpec((2, tile, out_cols), lambda i: (0, i, 0)),
        compiler_params=pltpu.CompilerParams(vmem_limit_bytes=16 << 20),
        cost_estimate=cost(4),
    )(place, maps, half, *[strips[c][k] for c, k in late])
    return result[None]


def solution(mesh):
    facets, cols = mesh.devices.shape
    fine = Mesh(
        mesh.devices.reshape(facets // 16, 2, 2, 4, cols), ("zq", "zp", "xl", "y", "col")
    )
    in_specs = (
        P(FACET, None, None, "col"),
        P(None, "col"),
        P(),
        P(),
        P(FACET, None, None, "col"),
    )
    out_specs = P(FACET, None, "col", None)
    return jax.shard_map(body, mesh=fine, in_specs=in_specs, out_specs=out_specs, check_vma=False)
```

```python
import math

import jax
import jax.numpy as jnp
import ml_dtypes
import numpy as np
from jax import lax
from jax.experimental import pallas as pl
from jax.experimental.pallas import tpu as pltpu
from jax.sharding import Mesh
from jax.sharding import PartitionSpec as P

XM = 128
LANES = 128
HALF = LANES // 2
BF16 = jnp.bfloat16
F32 = jnp.float32
FACET = ("zq", "zp", "xl", "y")
NEAR = (("zp", "xl", "y"), ("xl", "y"))
FAR = (("zq",), ("zq", "zp"))


def side_by_side(real_part, imag_part):
    return np.concatenate([real_part, imag_part], axis=1).astype(ml_dtypes.bfloat16)


def waves(length, sign_factor, scaling):
    positions = np.arange(length)
    angles = 2.0 * np.pi / length * ((positions[:, None] * positions[None, :]) % length)
    return np.cos(angles) * scaling, sign_factor * np.sin(angles) * scaling


def small_tables():
    taper = 0.3 + 0.7 * np.sin(np.pi * (np.arange(XM) + 0.5) / XM) ** 2
    fwd_re, fwd_im = waves(XM, -1.0, 1.0 / math.sqrt(XM))
    back_re, back_im = waves(XM, 1.0, 1.0 / math.sqrt(XM))
    forward = side_by_side(fwd_re * taper[None, :], fwd_im * taper[None, :])
    backward = side_by_side(back_re * taper[:, None], back_im * taper[:, None])
    return forward, backward


def grid_table(grid_len, facet_count):
    coarse = np.arange(0, grid_len, 16)[:, None] * np.arange(grid_len)[None, :] % grid_len
    fine = np.arange(16)[:, None] * np.arange(grid_len)[None, :] % grid_len
    scaling = 1.0 / math.sqrt(facet_count * XM)
    coarse = np.exp(-2j * np.pi * coarse / grid_len) * scaling
    fine = np.exp(-2j * np.pi * fine / grid_len)
    parts = [p.astype(np.float32) for p in (coarse.real, coarse.imag, fine.real, fine.imag)]
    c_re, c_im, f_re, f_im = lax.optimization_barrier(tuple(jnp.asarray(p) for p in parts))
    c_re, c_im = c_re[:, None, :], c_im[:, None, :]
    f_re, f_im = f_re[None, :, :], f_im[None, :, :]
    real_part = (c_re * f_re - c_im * f_im).reshape(grid_len, grid_len).astype(BF16)
    imag_part = (c_re * f_im + c_im * f_re).reshape(grid_len, grid_len).astype(BF16)
    return jnp.concatenate([real_part, imag_part], axis=1)


def finish_maps(columns, out_cols):
    frequency = jnp.arange(out_cols, dtype=jnp.int32)
    products = columns[:, :, None] * frequency[None, None, :] % out_cols
    angles = 2.0 * math.pi / out_cols * products.astype(F32)
    scaling = 1.0 / math.sqrt(2 * out_cols)
    real_part = jnp.cos(angles) * scaling
    imag_part = jnp.sin(angles) * scaling
    from_real = jnp.concatenate([real_part, imag_part], axis=2).astype(BF16)
    from_imag = jnp.concatenate([-imag_part, real_part], axis=2).astype(BF16)
    cols = columns.shape[0]
    shape = (cols, LANES // HALF, 1, HALF, 2 * out_cols)
    both = jnp.concatenate([from_real.reshape(shape), from_imag.reshape(shape)], axis=2)
    return both.transpose(1, 0, 2, 3, 4).reshape(LANES // HALF, cols, LANES, 2 * out_cols)


def low_half(shape):
    return lax.broadcasted_iota(jnp.int32, shape, len(shape) - 1) < HALF


def turn(block):
    swapped = pltpu.roll(block, HALF, 1)
    return jnp.where(low_half(block.shape), -swapped, swapped)


def pack(chunk, real_part, imag_part):
    if chunk == 0:
        return jnp.where(low_half(real_part.shape), real_part, pltpu.roll(imag_part, HALF, 1))
    return jnp.where(low_half(real_part.shape), pltpu.roll(real_part, HALF, 1), imag_part)


def stack_turned(blocks):
    tops = jnp.concatenate(blocks, axis=1)
    lows = jnp.concatenate([turn(b) for b in blocks], axis=1)
    return jnp.concatenate([tops, lows], axis=0).astype(BF16)


def window_rows(first_rows, item, length):
    return pl.ds(jnp.bitwise_and(first_rows[item], length - 1), XM)


def contrib_kernel(chunk, starts, strip, table, out, held, source, made_rows, in_sems, out_sems):
    facet_len = strip.shape[1]
    parts = in_sems.shape[0]
    share = facet_len // parts
    tile = 256

    def fetch(p):
        rows = pl.ds(p * share, share)
        return pltpu.make_async_copy(strip.at[:, rows, :], held.at[:, rows, :], in_sems.at[p])

    for p in range(parts):
        fetch(p).start()

    def fill(i, _):
        rows = pl.ds(pl.multiple_of(i * tile, tile), tile)
        source[rows, :] = pack(chunk, held[0, rows, :].astype(F32), held[1, rows, :].astype(F32))
        return 0

    for p in range(parts):
        fetch(p).wait()
        lax.fori_loop(p * (share // tile), (p + 1) * (share // tile), fill, 0)
    source[pl.ds(facet_len, XM), :] = source[pl.ds(0, XM), :]
    planes, depth = out.shape[0], out.shape[1]

    def send(k):
        return pltpu.make_async_copy(made_rows.at[:, k], out.at[:, k], out_sems.at[k])

    def one_group(k, _):
        for j in range(0, planes, 2):
            first = source[window_rows(starts, k * planes + j, facet_len), :]
            second = source[window_rows(starts, k * planes + j + 1, facet_len), :]
            made = jnp.dot(table[...], stack_turned([first, second]), preferred_element_type=F32)
            made_rows[j, k] = made[:, :LANES].astype(BF16)
            made_rows[j + 1, k] = made[:, LANES:].astype(BF16)
        send(k).start()
        return 0

    lax.fori_loop(0, depth, one_group, 0, unroll=2)
    for k in range(depth):
        send(k).wait()


def gather_kernel(chunk, place, offsets, arrived, *refs):
    *outs, held, total, sems = refs
    planes, depth = arrived.shape[0], arrived.shape[1]
    grid_len = total.shape[0] - XM
    owners = [lax.rem(place[chunk] + k * (1 if chunk == 0 else place[3]), depth) for k in range(depth)]

    def fetch(owner):
        return pltpu.make_async_copy(arrived.at[:, owner], held.at[:, owner], sems.at[owner])

    for owner in owners:
        fetch(owner).start()
    for owner, out in zip(owners, outs):
        total[...] = jnp.zeros_like(total)
        fetch(owner).wait()

        def one_facet(j, _, owner=owner):
            rows = window_rows(offsets, place[chunk] * planes + j, grid_len)
            total[rows, :] = total[rows, :] + held[j, owner].astype(F32)
            return 0

        lax.fori_loop(0, planes, one_facet, 0, unroll=8)
        total[pl.ds(0, XM), :] = total[pl.ds(0, XM), :] + total[pl.ds(grid_len, XM), :]
        base = out.shape[0] - grid_len
        out[pl.ds(base, grid_len), :] = total[pl.ds(0, grid_len), :].astype(BF16)
        if base > 0:
            out[pl.ds(0, base), :] = jnp.zeros((base, LANES), BF16)


def grid_kernel(chunk, weights, table, *refs):
    *parts, out = refs
    grid_len = weights.shape[1]
    total = 0.0
    for part in parts:
        total = total + part[pl.ds(part.shape[0] - grid_len, grid_len), :].astype(F32)
    assembled = total.astype(BF16).astype(F32)
    spectrum = jnp.dot(table[...], stack_turned([assembled]), preferred_element_type=F32)
    weight_re = weights[0].astype(F32)
    weight_im = weights[1].astype(F32)
    both_re = pack(chunk, weight_re, weight_re)
    both_im = pack(chunk, weight_im, weight_im)
    weighted = (both_re * spectrum + both_im * turn(spectrum)).astype(BF16).astype(F32)
    back = jnp.concatenate([weighted, -turn(weighted)], axis=0).astype(BF16)
    image = jnp.dot(table[...], back, preferred_element_type=F32)
    out[...] = (image * 4.0).astype(BF16)


def spread_kernel(place, offsets, *refs):
    *images, out, wide, made_rows, sems = refs
    grid_len = wide.shape[0] - XM
    planes = out.shape[0]

    def send(k):
        return pltpu.make_async_copy(made_rows.at[:, k], out.at[:, k], sems.at[k])

    for k, image in enumerate(images):
        wide[pl.ds(0, grid_len), :] = image[pl.ds(0, grid_len), :].astype(F32)
        wide[pl.ds(grid_len, XM), :] = wide[pl.ds(0, XM), :]

        def one_facet(j, _, k=k):
            rows = window_rows(offsets, place[1] * planes + j, grid_len)
            made_rows[j, k] = wide[rows, :].astype(BF16)
            return 0

        lax.fori_loop(0, planes, one_facet, 0, unroll=8)
        send(k).start()
    for k in range(len(images)):
        send(k).wait()


def accum_kernel(place, starts, returned, table, *refs):
    *outs, held, total, sems = refs
    planes, depth = returned.shape[0], returned.shape[1]
    own_rows = outs[0].shape[0]
    facet_len = own_rows * len(outs)

    def fetch(k):
        return pltpu.make_async_copy(returned.at[:, k], held.at[:, k], sems.at[k])

    for k in range(depth):
        fetch(k).start()
    total[...] = jnp.zeros_like(total)

    def one_group(k, _):
        fetch(k).wait()
        item = lax.rem(place[1] + k * (depth - place[3]), depth) * planes
        terms = []
        for j in range(0, planes, 2):
            blocks = [held[j, k].astype(F32), held[j + 1, k].astype(F32)]
            made = jnp.dot(table[...], stack_turned(blocks), preferred_element_type=F32)
            terms += [made[:, :LANES], made[:, LANES:]]
        for j, term in enumerate(terms):
            rows = window_rows(starts, item + j, facet_len)
            total[rows, :] = total[rows, :] + term
        return 0

    lax.fori_loop(0, depth, one_group, 0, unroll=2)
    total[pl.ds(0, XM), :] = total[pl.ds(0, XM), :] + total[pl.ds(facet_len, XM), :]
    tile = 256
    for k, out in enumerate(outs):
        first = jnp.bitwise_xor(place[2], k) * own_rows

        def drain(i, _, out=out, first=first):
            rows = pl.ds(pl.multiple_of(first + i * tile, tile), tile)
            out[pl.ds(pl.multiple_of(i * tile, tile), tile), :] = total[rows, :].astype(BF16)
            return 0

        lax.fori_loop(0, own_rows // tile, drain, 0)


def window(place, terms, maps):
    made = None
    for chunk, k, strip in terms:
        table = maps[chunk, jnp.bitwise_xor(place[2], k)]
        term = jnp.dot(strip[...], table, preferred_element_type=F32)
        made = term if made is None else made + term
    return made


def half_kernel(keys, place, maps, *strips_and_out):
    *strips, out = strips_and_out
    out[...] = window(place, [(*key, s) for key, s in zip(keys, strips)], maps)


def finish_kernel(keys, place, maps, made, *strips_and_out):
    *strips, out = strips_and_out
    out_cols = out.shape[2]
    both = made[...] + window(place, [(*key, s) for key, s in zip(keys, strips)], maps)
    out[0] = both[:, :out_cols].astype(BF16)
    out[1] = both[:, out_cols:].astype(BF16)


SMEM = pl.BlockSpec(memory_space=pltpu.SMEM)
VMEM = pl.BlockSpec(memory_space=pltpu.VMEM)
HBM = pl.BlockSpec(memory_space=pltpu.HBM)


def call(kernel, name, outs, in_specs, scratch, micros, limit, where=VMEM):
    made = jax.ShapeDtypeStruct if where is VMEM else pltpu.HBM
    shapes = [made(s, BF16) for s in outs]
    one = len(outs) == 1
    return pl.pallas_call(
        kernel,
        name=name,
        out_shape=shapes[0] if one else shapes,
        in_specs=in_specs,
        out_specs=where if one else [where] * len(outs),
        scratch_shapes=scratch,
        compiler_params=pltpu.CompilerParams(vmem_limit_bytes=limit << 20),
        cost_estimate=cost(micros),
    )


def cost(micros):
    return pl.CostEstimate(flops=0, bytes_accessed=int(micros * 3.5e6), transcendentals=0)


def bind(kernel, chunk):
    def bound(*refs):
        kernel(chunk, *refs)

    return bound


def shifted(value, step):
    size = lax.axis_size("zq")
    return lax.ppermute(value, "zq", [(i, (i + step) % size) for i in range(size)])


def turned(value, step):
    size, cols = lax.axis_size(FAR[1]), lax.axis_size("col")
    perm = [
        (i * cols + c, (i + (step if c % 2 == 0 else -step)) % size * cols + c)
        for i in range(size)
        for c in range(cols)
    ]
    return lax.ppermute(value, (*FAR[1], "col"), perm)


def swapped(value, flip):
    return lax.ppermute(value, "col", [(i, i ^ flip) for i in range(lax.axis_size("col"))])


def add(first, second):
    return (first.astype(F32) + second.astype(F32)).astype(BF16)


def body(prepared, sub_off, fac_off, win_col, vis_weights):
    facet_count = fac_off.shape[0]
    strip = prepared[0]
    weights = vis_weights[0]
    facet_len = strip.shape[1]
    grid_len = weights.shape[1]
    col_count = lax.axis_size("col")
    own_rows = facet_len // col_count
    out_cols = LANES * col_count // 2
    place = [lax.axis_index(FAR[0]), lax.axis_index(FAR[1]), lax.axis_index("col")]
    size = lax.axis_size(FAR[1])
    place.append(jnp.where(place[2] % 2 == 0, 1, size - 1))
    place = jnp.stack(place).astype(jnp.int32)
    starts = sub_off.reshape(-1)
    forward_small, backward_small = small_tables()
    grid_forward = grid_table(grid_len, facet_count)
    flips = sorted(range(1, col_count), reverse=True)
    long_rows = pltpu.VMEM((facet_len + XM, LANES), F32)
    grid_rows = pltpu.VMEM((grid_len + XM, LANES), F32)
    planes = [lax.axis_size(axes) for axes in NEAR]
    depths = [lax.axis_size(axes) for axes in FAR]
    blocks = [(p, d, XM, LANES) for p, d in zip(planes, depths)]
    held = [pltpu.VMEM(b, BF16) for b in blocks]
    sems = [pltpu.SemaphoreType.DMA((d,)) for d in depths]

    def contrib(c, strip):
        return call(
            bind(contrib_kernel, c), f"contrib{c}", [blocks[c]], [SMEM, HBM, VMEM],
            [pltpu.VMEM(strip.shape, BF16), long_rows, held[c], pltpu.SemaphoreType.DMA((8,)), sems[c]],
            8, 63, HBM,
        )(starts, strip, forward_small)

    def near(c, value):
        return lax.all_to_all(value, NEAR[c], 0, 0, tiled=True)

    def gather(c, arrived, doubled):
        outs = [(grid_len * (1 + (k in doubled)), LANES) for k in range(depths[c])]
        return call(
            bind(gather_kernel, c), f"gather{c}", outs,
            [SMEM, SMEM, HBM], [held[c], grid_rows, sems[c]], 2, 8,
        )(place, fac_off, arrived)

    def image_of(c, parts):
        return call(
            bind(grid_kernel, c), f"grid{c}", [(grid_len, LANES)], [VMEM] * (2 + len(parts)),
            [], 1.5, 12,
        )(weights, grid_forward, *parts)

    def spread(c, images):
        return call(
            spread_kernel, f"spread{c}", [blocks[1]], [SMEM, SMEM] + [VMEM] * depths[1],
            [grid_rows, held[1], sems[1]], 2, 8, HBM,
        )(place, fac_off, *images)

    def accum(c, returned):
        return call(
            accum_kernel, f"accum{c}", [(own_rows, LANES)] * col_count,
            [SMEM, SMEM, HBM, VMEM], [held[1], long_rows, sems[1]], 5, 14,
        )(place, starts, returned, backward_small)

    def exchange(summed):
        moved = {k: swapped(summed[k], k) for k in flips}
        return [summed[0]] + [moved[k] for k in range(1, col_count)]

    barrier = lax.optimization_barrier
    maps = finish_maps(win_col, out_cols)
    payload0 = contrib(0, strip)
    payload0, strip = barrier((payload0, strip))
    arrived0 = near(0, payload0)
    payload1 = contrib(1, strip)
    arrived0, payload1, maps, grid_forward = barrier((arrived0, payload1, maps, grid_forward))
    arrived1 = near(1, payload1)

    steps = sorted(range(1, depths[0]), key=lambda k: -min(k, depths[0] - k))
    parts0 = gather(0, arrived0, ())
    image0 = image_of(0, [parts0[0]] + [shifted(parts0[k], k) for k in steps])

    far, near_side = depths[1] // 2, (depths[1] - 1) // 2
    doubled = [*range(2, far), *range(far + 2, depths[1] - 1)]
    parts1 = gather(1, arrived1, doubled)
    ups, downs = [turned(image0, 1)], [turned(image0, -1)]
    up = jnp.concatenate([ups[0], parts1[far]])
    down = jnp.concatenate([downs[0], parts1[far + 1]])
    for i in range(far - 1):
        up = turned(up, 1)
        ups.append(up)
        if i < far - 2:
            up = add(up, parts1[far - 1 - i])
    for i in range(near_side - 1):
        down = turned(down, -1)
        downs.append(down)
        if i < near_side - 2:
            down = add(down, parts1[far + 2 + i])
    up = turned(add(up[grid_len:], parts1[1]), 1)
    down = turned(add(down[grid_len:], parts1[depths[1] - 1]), -1)
    images0 = [image0] + ups + downs[::-1]
    image1 = image_of(1, [parts1[0], up, down])
    images0[0], image1 = barrier((image0, image1))
    returned0 = near(1, spread(0, images0))

    ups, downs = [image1], [image1]
    for i in range(far):
        ups.append(turned(ups[-1], 1))
        if i < near_side:
            downs.append(turned(downs[-1], -1))
    spread1 = spread(1, ups + downs[:0:-1])
    returned0, spread1 = barrier((returned0, spread1))
    returned1 = near(1, spread1)
    accum0 = accum(0, returned0)
    strips0 = exchange(accum0)
    strips1 = exchange(accum(1, returned1))

    tile = min(512, own_rows)
    strip_spec = pl.BlockSpec((tile, LANES), lambda i: (i, 0))
    maps_spec = pl.BlockSpec(maps.shape, lambda i: (0, 0, 0, 0))
    wide_spec = pl.BlockSpec((tile, 2 * out_cols), lambda i: (i, 0))
    late = [(1, k) for k in range(2, col_count)]
    early = [(0, k) for k in range(col_count)] + [(1, 0), (1, 1)]
    strips = (strips0, strips1)
    half = pl.pallas_call(
        bind(half_kernel, early),
        name="half",
        grid=(own_rows // tile,),
        out_shape=jax.ShapeDtypeStruct((own_rows, 2 * out_cols), F32),
        in_specs=[SMEM, maps_spec] + [strip_spec] * len(early),
        out_specs=wide_spec,
        compiler_params=pltpu.CompilerParams(vmem_limit_bytes=16 << 20),
        cost_estimate=cost(4),
    )(place, maps, *[strips[c][k] for c, k in early])
    result = pl.pallas_call(
        bind(finish_kernel, late),
        name="finish",
        grid=(own_rows // tile,),
        out_shape=jax.ShapeDtypeStruct((2, own_rows, out_cols), BF16),
        in_specs=[SMEM, maps_spec, wide_spec] + [strip_spec] * len(late),
        out_specs=pl.BlockSpec((2, tile, out_cols), lambda i: (0, i, 0)),
        compiler_params=pltpu.CompilerParams(vmem_limit_bytes=16 << 20),
        cost_estimate=cost(4),
    )(place, maps, half, *[strips[c][k] for c, k in late])
    return result[None]


def solution(mesh):
    facets, cols = mesh.devices.shape
    fine = Mesh(
        mesh.devices.reshape(facets // 16, 2, 2, 4, cols), ("zq", "zp", "xl", "y", "col")
    )
    in_specs = (
        P(FACET, None, None, "col"),
        P(None, "col"),
        P(),
        P(),
        P(FACET, None, None, "col"),
    )
    out_specs = P(FACET, None, "col", None)
    return jax.shard_map(body, mesh=fine, in_specs=in_specs, out_specs=out_specs, check_vma=False)
```

```python
import math

import jax
import jax.numpy as jnp
import ml_dtypes
import numpy as np
from jax import lax
from jax.experimental import pallas as pl
from jax.experimental.pallas import tpu as pltpu
from jax.sharding import Mesh
from jax.sharding import PartitionSpec as P

XM = 128
LANES = 128
HALF = LANES // 2
BF16 = jnp.bfloat16
F32 = jnp.float32
FACET = ("zq", "zp", "xl", "y")
NEAR = (("zp", "xl", "y"), ("xl", "y"))
FAR = (("zq",), ("zq", "zp"))


def side_by_side(real_part, imag_part):
    return np.concatenate([real_part, imag_part], axis=1).astype(ml_dtypes.bfloat16)


def waves(length, sign_factor, scaling):
    positions = np.arange(length)
    angles = 2.0 * np.pi / length * ((positions[:, None] * positions[None, :]) % length)
    return np.cos(angles) * scaling, sign_factor * np.sin(angles) * scaling


def small_tables():
    taper = 0.3 + 0.7 * np.sin(np.pi * (np.arange(XM) + 0.5) / XM) ** 2
    fwd_re, fwd_im = waves(XM, -1.0, 1.0 / math.sqrt(XM))
    back_re, back_im = waves(XM, 1.0, 1.0 / math.sqrt(XM))
    forward = side_by_side(fwd_re * taper[None, :], fwd_im * taper[None, :])
    backward = side_by_side(back_re * taper[:, None], back_im * taper[:, None])
    return forward, backward


def grid_table(grid_len, facet_count):
    coarse = np.arange(0, grid_len, 16)[:, None] * np.arange(grid_len)[None, :] % grid_len
    fine = np.arange(16)[:, None] * np.arange(grid_len)[None, :] % grid_len
    scaling = 1.0 / math.sqrt(facet_count * XM)
    coarse = np.exp(-2j * np.pi * coarse / grid_len) * scaling
    fine = np.exp(-2j * np.pi * fine / grid_len)
    parts = [p.astype(np.float32) for p in (coarse.real, coarse.imag, fine.real, fine.imag)]
    c_re, c_im, f_re, f_im = lax.optimization_barrier(tuple(jnp.asarray(p) for p in parts))
    c_re, c_im = c_re[:, None, :], c_im[:, None, :]
    f_re, f_im = f_re[None, :, :], f_im[None, :, :]
    real_part = (c_re * f_re - c_im * f_im).reshape(grid_len, grid_len).astype(BF16)
    imag_part = (c_re * f_im + c_im * f_re).reshape(grid_len, grid_len).astype(BF16)
    return jnp.concatenate([real_part, imag_part], axis=1)


def finish_maps(columns, out_cols):
    frequency = jnp.arange(out_cols, dtype=jnp.int32)
    products = columns[:, :, None] * frequency[None, None, :] % out_cols
    angles = 2.0 * math.pi / out_cols * products.astype(F32)
    scaling = 1.0 / math.sqrt(2 * out_cols)
    real_part = jnp.cos(angles) * scaling
    imag_part = jnp.sin(angles) * scaling
    from_real = jnp.concatenate([real_part, imag_part], axis=2).astype(BF16)
    from_imag = jnp.concatenate([-imag_part, real_part], axis=2).astype(BF16)
    cols = columns.shape[0]
    shape = (cols, LANES // HALF, 1, HALF, 2 * out_cols)
    both = jnp.concatenate([from_real.reshape(shape), from_imag.reshape(shape)], axis=2)
    return both.transpose(1, 0, 2, 3, 4).reshape(LANES // HALF, cols, LANES, 2 * out_cols)


def low_half(shape):
    return lax.broadcasted_iota(jnp.int32, shape, len(shape) - 1) < HALF


def turn(block):
    swapped = pltpu.roll(block, HALF, 1)
    return jnp.where(low_half(block.shape), -swapped, swapped)


def pack(chunk, real_part, imag_part):
    if chunk == 0:
        return jnp.where(low_half(real_part.shape), real_part, pltpu.roll(imag_part, HALF, 1))
    return jnp.where(low_half(real_part.shape), pltpu.roll(real_part, HALF, 1), imag_part)


def stack_turned(blocks):
    tops = jnp.concatenate(blocks, axis=1)
    lows = jnp.concatenate([turn(b) for b in blocks], axis=1)
    return jnp.concatenate([tops, lows], axis=0).astype(BF16)


def window_rows(first_rows, item, length):
    return pl.ds(jnp.bitwise_and(first_rows[item], length - 1), XM)


def contrib_kernel(chunk, starts, strip, table, out, held, source, made_rows, in_sems, out_sems):
    facet_len = strip.shape[1]
    parts = in_sems.shape[0]
    share = facet_len // parts
    tile = 256

    def fetch(p):
        rows = pl.ds(p * share, share)
        return pltpu.make_async_copy(strip.at[:, rows, :], held.at[:, rows, :], in_sems.at[p])

    for p in range(parts):
        fetch(p).start()

    def fill(i, _):
        rows = pl.ds(pl.multiple_of(i * tile, tile), tile)
        source[rows, :] = pack(chunk, held[0, rows, :].astype(F32), held[1, rows, :].astype(F32))
        return 0

    for p in range(parts):
        fetch(p).wait()
        lax.fori_loop(p * (share // tile), (p + 1) * (share // tile), fill, 0)
    source[pl.ds(facet_len, XM), :] = source[pl.ds(0, XM), :]
    planes, depth = out.shape[0], out.shape[1]

    def send(k):
        return pltpu.make_async_copy(made_rows.at[:, k], out.at[:, k], out_sems.at[k])

    def one_group(k, _):
        for j in range(0, planes, 2):
            first = source[window_rows(starts, k * planes + j, facet_len), :]
            second = source[window_rows(starts, k * planes + j + 1, facet_len), :]
            made = jnp.dot(table[...], stack_turned([first, second]), preferred_element_type=F32)
            made_rows[j, k] = made[:, :LANES].astype(BF16)
            made_rows[j + 1, k] = made[:, LANES:].astype(BF16)
        send(k).start()
        return 0

    lax.fori_loop(0, depth, one_group, 0, unroll=4)
    for k in range(depth):
        send(k).wait()


def gather_kernel(chunk, ks, place, offsets, arrived, *refs):
    *outs, held, total, sems = refs
    planes, depth = arrived.shape[0], arrived.shape[1]
    grid_len = total.shape[0] - XM
    stride = 1 if chunk == 0 else place[3]
    owners = [lax.rem(place[chunk] + k * stride, depth) for k in ks]

    def fetch(owner):
        return pltpu.make_async_copy(arrived.at[:, owner], held.at[:, owner], sems.at[owner])

    for owner in owners:
        fetch(owner).start()
    for owner, out in zip(owners, outs):
        total[...] = jnp.zeros_like(total)
        fetch(owner).wait()

        def one_facet(j, _, owner=owner):
            rows = window_rows(offsets, place[chunk] * planes + j, grid_len)
            total[rows, :] = total[rows, :] + held[j, owner].astype(F32)
            return 0

        lax.fori_loop(0, planes, one_facet, 0, unroll=8)
        total[pl.ds(0, XM), :] = total[pl.ds(0, XM), :] + total[pl.ds(grid_len, XM), :]
        base = out.shape[0] - grid_len
        out[pl.ds(base, grid_len), :] = total[pl.ds(0, grid_len), :].astype(BF16)
        if base > 0:
            out[pl.ds(0, base), :] = jnp.zeros((base, LANES), BF16)


def grid_kernel(chunk, weights, table, *refs):
    *parts, out = refs
    grid_len = weights.shape[1]
    total = 0.0
    for part in parts:
        total = total + part[pl.ds(part.shape[0] - grid_len, grid_len), :].astype(F32)
    assembled = total.astype(BF16).astype(F32)
    spectrum = jnp.dot(table[...], stack_turned([assembled]), preferred_element_type=F32)
    weight_re = weights[0].astype(F32)
    weight_im = weights[1].astype(F32)
    both_re = pack(chunk, weight_re, weight_re)
    both_im = pack(chunk, weight_im, weight_im)
    weighted = (both_re * spectrum + both_im * turn(spectrum)).astype(BF16).astype(F32)
    back = jnp.concatenate([weighted, -turn(weighted)], axis=0).astype(BF16)
    image = jnp.dot(table[...], back, preferred_element_type=F32)
    out[...] = (image * 4.0).astype(BF16)


def spread_kernel(place, offsets, *refs):
    *images, out, wide, made_rows, sems = refs
    grid_len = wide.shape[0] - XM
    planes = out.shape[0]

    def send(k):
        return pltpu.make_async_copy(made_rows.at[:, k], out.at[:, k], sems.at[k])

    for k, image in enumerate(images):
        wide[pl.ds(0, grid_len), :] = image[pl.ds(0, grid_len), :].astype(F32)
        wide[pl.ds(grid_len, XM), :] = wide[pl.ds(0, XM), :]

        def one_facet(j, _, k=k):
            rows = window_rows(offsets, place[1] * planes + j, grid_len)
            made_rows[j, k] = wide[rows, :].astype(BF16)
            return 0

        lax.fori_loop(0, planes, one_facet, 0, unroll=8)
        send(k).start()
    for k in range(len(images)):
        send(k).wait()


def accum_kernel(place, starts, returned, table, *refs):
    *outs, held, total, sems = refs
    planes, depth = returned.shape[0], returned.shape[1]
    own_rows = outs[0].shape[0]
    facet_len = own_rows * len(outs)

    def fetch(k):
        return pltpu.make_async_copy(returned.at[:, k], held.at[:, k], sems.at[k])

    for k in range(depth):
        fetch(k).start()
    total[...] = jnp.zeros_like(total)

    def one_group(k, _):
        fetch(k).wait()
        item = lax.rem(place[1] + k * (depth - place[3]), depth) * planes
        terms = []
        for j in range(0, planes, 2):
            blocks = [held[j, k].astype(F32), held[j + 1, k].astype(F32)]
            made = jnp.dot(table[...], stack_turned(blocks), preferred_element_type=F32)
            terms += [made[:, :LANES], made[:, LANES:]]
        for j, term in enumerate(terms):
            rows = window_rows(starts, item + j, facet_len)
            total[rows, :] = total[rows, :] + term
        return 0

    lax.fori_loop(0, depth, one_group, 0, unroll=2)
    total[pl.ds(0, XM), :] = total[pl.ds(0, XM), :] + total[pl.ds(facet_len, XM), :]
    tile = 256
    for k, out in enumerate(outs):
        first = jnp.bitwise_xor(place[2], k) * own_rows

        def drain(i, _, out=out, first=first):
            rows = pl.ds(pl.multiple_of(first + i * tile, tile), tile)
            out[pl.ds(pl.multiple_of(i * tile, tile), tile), :] = total[rows, :].astype(BF16)
            return 0

        lax.fori_loop(0, own_rows // tile, drain, 0)


def window(place, terms, maps):
    made = None
    for chunk, k, strip in terms:
        table = maps[chunk, jnp.bitwise_xor(place[2], k)]
        term = jnp.dot(strip[...], table, preferred_element_type=F32)
        made = term if made is None else made + term
    return made


def half_kernel(keys, place, maps, *strips_and_out):
    *strips, out = strips_and_out
    out[...] = window(place, [(*key, s) for key, s in zip(keys, strips)], maps)


def finish_kernel(keys, place, maps, made, *strips_and_out):
    *strips, out = strips_and_out
    out_cols = out.shape[2]
    both = made[...] + window(place, [(*key, s) for key, s in zip(keys, strips)], maps)
    out[0] = both[:, :out_cols].astype(BF16)
    out[1] = both[:, out_cols:].astype(BF16)


SMEM = pl.BlockSpec(memory_space=pltpu.SMEM)
VMEM = pl.BlockSpec(memory_space=pltpu.VMEM)
HBM = pl.BlockSpec(memory_space=pltpu.HBM)


def call(kernel, name, outs, in_specs, scratch, micros, limit, where=VMEM):
    made = jax.ShapeDtypeStruct if where is VMEM else pltpu.HBM
    shapes = [made(s, BF16) for s in outs]
    one = len(outs) == 1
    return pl.pallas_call(
        kernel,
        name=name,
        out_shape=shapes[0] if one else shapes,
        in_specs=in_specs,
        out_specs=where if one else [where] * len(outs),
        scratch_shapes=scratch,
        compiler_params=pltpu.CompilerParams(vmem_limit_bytes=limit << 20),
        cost_estimate=cost(micros),
    )


def cost(micros):
    return pl.CostEstimate(flops=0, bytes_accessed=int(micros * 3.5e6), transcendentals=0)


def bind(kernel, chunk):
    def bound(*refs):
        kernel(chunk, *refs)

    return bound


def shifted(value, step):
    size = lax.axis_size("zq")
    return lax.ppermute(value, "zq", [(i, (i + step) % size) for i in range(size)])


def turned(value, step):
    size, cols = lax.axis_size(FAR[1]), lax.axis_size("col")
    perm = [
        (i * cols + c, (i + (step if c % 2 == 0 else -step)) % size * cols + c)
        for i in range(size)
        for c in range(cols)
    ]
    return lax.ppermute(value, (*FAR[1], "col"), perm)


def swapped(value, flip):
    return lax.ppermute(value, "col", [(i, i ^ flip) for i in range(lax.axis_size("col"))])


def add(first, second):
    return (first.astype(F32) + second.astype(F32)).astype(BF16)


def body(prepared, sub_off, fac_off, win_col, vis_weights):
    facet_count = fac_off.shape[0]
    strip = prepared[0]
    weights = vis_weights[0]
    facet_len = strip.shape[1]
    grid_len = weights.shape[1]
    col_count = lax.axis_size("col")
    own_rows = facet_len // col_count
    out_cols = LANES * col_count // 2
    place = [lax.axis_index(FAR[0]), lax.axis_index(FAR[1]), lax.axis_index("col")]
    size = lax.axis_size(FAR[1])
    place.append(jnp.where(place[2] % 2 == 0, 1, size - 1))
    place = jnp.stack(place).astype(jnp.int32)
    starts = sub_off.reshape(-1)
    forward_small, backward_small = small_tables()
    grid_forward = grid_table(grid_len, facet_count)
    flips = sorted(range(1, col_count), reverse=True)
    long_rows = pltpu.VMEM((facet_len + XM, LANES), F32)
    grid_rows = pltpu.VMEM((grid_len + XM, LANES), F32)
    planes = [lax.axis_size(axes) for axes in NEAR]
    depths = [lax.axis_size(axes) for axes in FAR]
    blocks = [(p, d, XM, LANES) for p, d in zip(planes, depths)]
    held = [pltpu.VMEM(b, BF16) for b in blocks]
    sems = [pltpu.SemaphoreType.DMA((d,)) for d in depths]

    def contrib(c, strip):
        return call(
            bind(contrib_kernel, c), f"contrib{c}", [blocks[c]], [SMEM, HBM, VMEM],
            [pltpu.VMEM(strip.shape, BF16), long_rows, held[c], pltpu.SemaphoreType.DMA((8,)), sems[c]],
            8, 63, HBM,
        )(starts, strip, forward_small)

    def near(c, value):
        return lax.all_to_all(value, NEAR[c], 0, 0, tiled=True)

    def gather(c, arrived, ks, doubled):
        outs = [(grid_len * (1 + (k in doubled)), LANES) for k in ks]
        made = call(
            lambda *refs: gather_kernel(c, ks, *refs), f"gather{c}{ks[0]}", outs,
            [SMEM, SMEM, HBM], [held[c], grid_rows, sems[c]], 1, 8,
        )(place, fac_off, arrived)
        return dict(zip(ks, made))

    def image_of(c, parts):
        return call(
            bind(grid_kernel, c), f"grid{c}", [(grid_len, LANES)], [VMEM] * (2 + len(parts)),
            [], 1.5, 12,
        )(weights, grid_forward, *parts)

    def spread(c, images):
        return call(
            spread_kernel, f"spread{c}", [blocks[1]], [SMEM, SMEM] + [VMEM] * depths[1],
            [grid_rows, held[1], sems[1]], 2, 8, HBM,
        )(place, fac_off, *images)

    def accum(c, returned):
        return call(
            accum_kernel, f"accum{c}", [(own_rows, LANES)] * col_count,
            [SMEM, SMEM, HBM, VMEM], [held[1], long_rows, sems[1]], 5, 14,
        )(place, starts, returned, backward_small)

    def exchange(summed):
        moved = {k: swapped(summed[k], k) for k in flips}
        return [summed[0]] + [moved[k] for k in range(1, col_count)]

    barrier = lax.optimization_barrier
    maps = finish_maps(win_col, out_cols)
    payload0 = contrib(0, strip)
    payload0, strip = barrier((payload0, strip))
    arrived0 = near(0, payload0)
    payload1 = contrib(1, strip)
    arrived0, payload1, maps, grid_forward = barrier((arrived0, payload1, maps, grid_forward))
    arrived1 = near(1, payload1)

    steps = sorted(range(1, depths[0]), key=lambda k: -min(k, depths[0] - k))
    parts0 = gather(0, arrived0, [*range(depths[0])], ())
    image0 = image_of(0, [parts0[0]] + [shifted(parts0[k], k) for k in steps])

    far, near_side = depths[1] // 2, (depths[1] - 1) // 2
    doubled = [*range(2, far), *range(far + 2, depths[1] - 1)]
    first = [far, far + 1]
    parts1 = gather(1, arrived1, first, ())
    parts1 |= gather(1, arrived1, [k for k in range(depths[1]) if k not in first], doubled)
    ups, downs = barrier(([turned(image0, 1)], [turned(image0, -1)]))
    up = jnp.concatenate([ups[0], parts1[far]])
    down = jnp.concatenate([downs[0], parts1[far + 1]])
    for i in range(far - 1):
        up = turned(up, 1)
        ups.append(up)
        if i < far - 2:
            up = add(up, parts1[far - 1 - i])
    for i in range(near_side - 1):
        down = turned(down, -1)
        downs.append(down)
        if i < near_side - 2:
            down = add(down, parts1[far + 2 + i])
    up = turned(add(up[grid_len:], parts1[1]), 1)
    down = turned(add(down[grid_len:], parts1[depths[1] - 1]), -1)
    images0 = [image0] + ups + downs[::-1]
    image1 = image_of(1, [parts1[0], up, down])
    images0[0], image1 = barrier((image0, image1))
    returned0 = near(1, spread(0, images0))

    ups, downs = [image1], [image1]
    for i in range(far):
        ups.append(turned(ups[-1], 1))
        if i < near_side:
            downs.append(turned(downs[-1], -1))
    spread1 = spread(1, ups + downs[:0:-1])
    returned0, spread1 = barrier((returned0, spread1))
    returned1 = near(1, spread1)
    accum0 = accum(0, returned0)
    strips0 = exchange(accum0)
    strips1 = exchange(accum(1, returned1))

    tile = min(512, own_rows)
    strip_spec = pl.BlockSpec((tile, LANES), lambda i: (i, 0))
    maps_spec = pl.BlockSpec(maps.shape, lambda i: (0, 0, 0, 0))
    wide_spec = pl.BlockSpec((tile, 2 * out_cols), lambda i: (i, 0))
    late = [(1, k) for k in range(2, col_count)]
    early = [(0, k) for k in range(col_count)] + [(1, 0), (1, 1)]
    strips = (strips0, strips1)
    half = pl.pallas_call(
        bind(half_kernel, early),
        name="half",
        grid=(own_rows // tile,),
        out_shape=jax.ShapeDtypeStruct((own_rows, 2 * out_cols), F32),
        in_specs=[SMEM, maps_spec] + [strip_spec] * len(early),
        out_specs=wide_spec,
        compiler_params=pltpu.CompilerParams(vmem_limit_bytes=16 << 20),
        cost_estimate=cost(4),
    )(place, maps, *[strips[c][k] for c, k in early])
    result = pl.pallas_call(
        bind(finish_kernel, late),
        name="finish",
        grid=(own_rows // tile,),
        out_shape=jax.ShapeDtypeStruct((2, own_rows, out_cols), BF16),
        in_specs=[SMEM, maps_spec, wide_spec] + [strip_spec] * len(late),
        out_specs=pl.BlockSpec((2, tile, out_cols), lambda i: (0, i, 0)),
        compiler_params=pltpu.CompilerParams(vmem_limit_bytes=16 << 20),
        cost_estimate=cost(4),
    )(place, maps, half, *[strips[c][k] for c, k in late])
    return result[None]


def solution(mesh):
    facets, cols = mesh.devices.shape
    fine = Mesh(
        mesh.devices.reshape(facets // 16, 2, 2, 4, cols), ("zq", "zp", "xl", "y", "col")
    )
    in_specs = (
        P(FACET, None, None, "col"),
        P(None, "col"),
        P(),
        P(),
        P(FACET, None, None, "col"),
    )
    out_specs = P(FACET, None, "col", None)
    return jax.shard_map(body, mesh=fine, in_specs=in_specs, out_specs=out_specs, check_vma=False)
```

```python
import math

import jax
import jax.numpy as jnp
import ml_dtypes
import numpy as np
from jax import lax
from jax.experimental import pallas as pl
from jax.experimental.pallas import tpu as pltpu
from jax.sharding import Mesh
from jax.sharding import PartitionSpec as P

XM = 128
LANES = 128
HALF = LANES // 2
BF16 = jnp.bfloat16
F32 = jnp.float32
FACET = ("zq", "zp", "xl", "y")
NEAR = (("zp", "xl", "y"), ("xl", "y"))
FAR = (("zq",), ("zq", "zp"))


def side_by_side(real_part, imag_part):
    return np.concatenate([real_part, imag_part], axis=1).astype(ml_dtypes.bfloat16)


def waves(length, sign_factor, scaling):
    positions = np.arange(length)
    angles = 2.0 * np.pi / length * ((positions[:, None] * positions[None, :]) % length)
    return np.cos(angles) * scaling, sign_factor * np.sin(angles) * scaling


def small_tables():
    taper = 0.3 + 0.7 * np.sin(np.pi * (np.arange(XM) + 0.5) / XM) ** 2
    fwd_re, fwd_im = waves(XM, -1.0, 1.0 / math.sqrt(XM))
    back_re, back_im = waves(XM, 1.0, 1.0 / math.sqrt(XM))
    forward = side_by_side(fwd_re * taper[None, :], fwd_im * taper[None, :])
    backward = side_by_side(back_re * taper[:, None], back_im * taper[:, None])
    return forward, backward


def grid_table(grid_len, facet_count):
    coarse = np.arange(0, grid_len, 16)[:, None] * np.arange(grid_len)[None, :] % grid_len
    fine = np.arange(16)[:, None] * np.arange(grid_len)[None, :] % grid_len
    scaling = 1.0 / math.sqrt(facet_count * XM)
    coarse = np.exp(-2j * np.pi * coarse / grid_len) * scaling
    fine = np.exp(-2j * np.pi * fine / grid_len)
    parts = [p.astype(np.float32) for p in (coarse.real, coarse.imag, fine.real, fine.imag)]
    c_re, c_im, f_re, f_im = lax.optimization_barrier(tuple(jnp.asarray(p) for p in parts))
    c_re, c_im = c_re[:, None, :], c_im[:, None, :]
    f_re, f_im = f_re[None, :, :], f_im[None, :, :]
    real_part = (c_re * f_re - c_im * f_im).reshape(grid_len, grid_len).astype(BF16)
    imag_part = (c_re * f_im + c_im * f_re).reshape(grid_len, grid_len).astype(BF16)
    return jnp.concatenate([real_part, imag_part], axis=1)


def finish_maps(columns, out_cols):
    frequency = jnp.arange(out_cols, dtype=jnp.int32)
    products = columns[:, :, None] * frequency[None, None, :] % out_cols
    angles = 2.0 * math.pi / out_cols * products.astype(F32)
    scaling = 1.0 / math.sqrt(2 * out_cols)
    real_part = jnp.cos(angles) * scaling
    imag_part = jnp.sin(angles) * scaling
    from_real = jnp.concatenate([real_part, imag_part], axis=2).astype(BF16)
    from_imag = jnp.concatenate([-imag_part, real_part], axis=2).astype(BF16)
    cols = columns.shape[0]
    shape = (cols, LANES // HALF, 1, HALF, 2 * out_cols)
    both = jnp.concatenate([from_real.reshape(shape), from_imag.reshape(shape)], axis=2)
    return both.transpose(1, 0, 2, 3, 4).reshape(LANES // HALF, cols, LANES, 2 * out_cols)


def low_half(shape):
    return lax.broadcasted_iota(jnp.int32, shape, len(shape) - 1) < HALF


def turn(block):
    swapped = pltpu.roll(block, HALF, 1)
    return jnp.where(low_half(block.shape), -swapped, swapped)


def pack(chunk, real_part, imag_part):
    if chunk == 0:
        return jnp.where(low_half(real_part.shape), real_part, pltpu.roll(imag_part, HALF, 1))
    return jnp.where(low_half(real_part.shape), pltpu.roll(real_part, HALF, 1), imag_part)


def stack_turned(blocks):
    tops = jnp.concatenate(blocks, axis=1)
    lows = jnp.concatenate([turn(b) for b in blocks], axis=1)
    return jnp.concatenate([tops, lows], axis=0).astype(BF16)


def window_rows(first_rows, item, length):
    return pl.ds(jnp.bitwise_and(first_rows[item], length - 1), XM)


def contrib_kernel(chunk, starts, strip, table, out, held, source, made_rows, in_sems, out_sems):
    facet_len = strip.shape[1]
    parts = in_sems.shape[0]
    share = facet_len // parts
    tile = 256

    def fetch(p):
        rows = pl.ds(p * share, share)
        return pltpu.make_async_copy(strip.at[:, rows, :], held.at[:, rows, :], in_sems.at[p])

    for p in range(parts):
        fetch(p).start()

    def fill(i, _):
        rows = pl.ds(pl.multiple_of(i * tile, tile), tile)
        source[rows, :] = pack(chunk, held[0, rows, :].astype(F32), held[1, rows, :].astype(F32))
        return 0

    for p in range(parts):
        fetch(p).wait()
        lax.fori_loop(p * (share // tile), (p + 1) * (share // tile), fill, 0)
    source[pl.ds(facet_len, XM), :] = source[pl.ds(0, XM), :]
    planes, depth = out.shape[0], out.shape[1]

    def send(k):
        return pltpu.make_async_copy(made_rows.at[:, k], out.at[:, k], out_sems.at[k])

    def one_group(k, _):
        for j in range(0, planes, 2):
            first = source[window_rows(starts, k * planes + j, facet_len), :]
            second = source[window_rows(starts, k * planes + j + 1, facet_len), :]
            made = jnp.dot(table[...], stack_turned([first, second]), preferred_element_type=F32)
            made_rows[j, k] = made[:, :LANES].astype(BF16)
            made_rows[j + 1, k] = made[:, LANES:].astype(BF16)
        send(k).start()
        return 0

    lax.fori_loop(0, depth, one_group, 0, unroll=4)
    for k in range(depth):
        send(k).wait()


def gather_kernel(chunk, ks, place, offsets, arrived, *refs):
    *outs, held, total, sems = refs
    planes, depth = arrived.shape[0], arrived.shape[1]
    grid_len = total.shape[0] - XM
    stride = 1 if chunk == 0 else place[3]
    owners = [lax.rem(place[chunk] + k * stride, depth) for k in ks]

    def fetch(owner):
        return pltpu.make_async_copy(arrived.at[:, owner], held.at[:, owner], sems.at[owner])

    for owner in owners:
        fetch(owner).start()
    for owner, out in zip(owners, outs):
        total[...] = jnp.zeros_like(total)
        fetch(owner).wait()

        def one_facet(j, _, owner=owner):
            rows = window_rows(offsets, place[chunk] * planes + j, grid_len)
            total[rows, :] = total[rows, :] + held[j, owner].astype(F32)
            return 0

        lax.fori_loop(0, planes, one_facet, 0, unroll=8)
        total[pl.ds(0, XM), :] = total[pl.ds(0, XM), :] + total[pl.ds(grid_len, XM), :]
        base = out.shape[0] - grid_len
        out[pl.ds(base, grid_len), :] = total[pl.ds(0, grid_len), :].astype(BF16)
        if base > 0:
            out[pl.ds(0, base), :] = jnp.zeros((base, LANES), BF16)


def grid_kernel(chunk, weights, table, *refs):
    *parts, out = refs
    grid_len = weights.shape[1]
    total = 0.0
    for part in parts:
        total = total + part[pl.ds(part.shape[0] - grid_len, grid_len), :].astype(F32)
    assembled = total.astype(BF16).astype(F32)
    spectrum = jnp.dot(table[...], stack_turned([assembled]), preferred_element_type=F32)
    weight_re = weights[0].astype(F32)
    weight_im = weights[1].astype(F32)
    both_re = pack(chunk, weight_re, weight_re)
    both_im = pack(chunk, weight_im, weight_im)
    weighted = (both_re * spectrum + both_im * turn(spectrum)).astype(BF16).astype(F32)
    back = jnp.concatenate([weighted, -turn(weighted)], axis=0).astype(BF16)
    image = jnp.dot(table[...], back, preferred_element_type=F32)
    out[...] = (image * 4.0).astype(BF16)


def spread_kernel(place, offsets, *refs):
    *images, out, wide, made_rows, sems = refs
    grid_len = wide.shape[0] - XM
    planes = out.shape[0]

    def send(k):
        return pltpu.make_async_copy(made_rows.at[:, k], out.at[:, k], sems.at[k])

    for k, image in enumerate(images):
        wide[pl.ds(0, grid_len), :] = image[pl.ds(0, grid_len), :].astype(F32)
        wide[pl.ds(grid_len, XM), :] = wide[pl.ds(0, XM), :]

        def one_facet(j, _, k=k):
            rows = window_rows(offsets, place[1] * planes + j, grid_len)
            made_rows[j, k] = wide[rows, :].astype(BF16)
            return 0

        lax.fori_loop(0, planes, one_facet, 0, unroll=8)
        send(k).start()
    for k in range(len(images)):
        send(k).wait()


def accum_kernel(place, starts, returned, table, *refs):
    *outs, held, total, sems = refs
    planes, depth = returned.shape[0], returned.shape[1]
    own_rows = outs[0].shape[0]
    facet_len = own_rows * len(outs)

    def fetch(k):
        return pltpu.make_async_copy(returned.at[:, k], held.at[:, k], sems.at[k])

    for k in range(depth):
        fetch(k).start()
    total[...] = jnp.zeros_like(total)

    def one_group(k, _):
        fetch(k).wait()
        item = lax.rem(place[1] + k * (depth - place[3]), depth) * planes
        terms = []
        for j in range(0, planes, 2):
            blocks = [held[j, k].astype(F32), held[j + 1, k].astype(F32)]
            made = jnp.dot(table[...], stack_turned(blocks), preferred_element_type=F32)
            terms += [made[:, :LANES], made[:, LANES:]]
        for j, term in enumerate(terms):
            rows = window_rows(starts, item + j, facet_len)
            total[rows, :] = total[rows, :] + term
        return 0

    lax.fori_loop(0, depth, one_group, 0, unroll=2)
    total[pl.ds(0, XM), :] = total[pl.ds(0, XM), :] + total[pl.ds(facet_len, XM), :]
    tile = 256
    for k, out in enumerate(outs):
        first = jnp.bitwise_xor(place[2], k) * own_rows

        def drain(i, _, out=out, first=first):
            rows = pl.ds(pl.multiple_of(first + i * tile, tile), tile)
            out[pl.ds(pl.multiple_of(i * tile, tile), tile), :] = total[rows, :].astype(BF16)
            return 0

        lax.fori_loop(0, own_rows // tile, drain, 0)


def window(place, terms, maps):
    made = None
    for chunk, k, strip in terms:
        table = maps[chunk, jnp.bitwise_xor(place[2], k)]
        term = jnp.dot(strip[...], table, preferred_element_type=F32)
        made = term if made is None else made + term
    return made


def half_kernel(keys, place, maps, *strips_and_out):
    *strips, out = strips_and_out
    out[...] = window(place, [(*key, s) for key, s in zip(keys, strips)], maps)


def finish_kernel(keys, place, maps, made, *strips_and_out):
    *strips, out = strips_and_out
    out_cols = out.shape[2]
    both = made[...] + window(place, [(*key, s) for key, s in zip(keys, strips)], maps)
    out[0] = both[:, :out_cols].astype(BF16)
    out[1] = both[:, out_cols:].astype(BF16)


SMEM = pl.BlockSpec(memory_space=pltpu.SMEM)
VMEM = pl.BlockSpec(memory_space=pltpu.VMEM)
HBM = pl.BlockSpec(memory_space=pltpu.HBM)


def call(kernel, name, outs, in_specs, scratch, micros, limit, where=VMEM):
    made = jax.ShapeDtypeStruct if where is VMEM else pltpu.HBM
    shapes = [made(s, BF16) for s in outs]
    one = len(outs) == 1
    return pl.pallas_call(
        kernel,
        name=name,
        out_shape=shapes[0] if one else shapes,
        in_specs=in_specs,
        out_specs=where if one else [where] * len(outs),
        scratch_shapes=scratch,
        compiler_params=pltpu.CompilerParams(vmem_limit_bytes=limit << 20),
        cost_estimate=cost(micros),
    )


def cost(micros):
    return pl.CostEstimate(flops=0, bytes_accessed=int(micros * 3.5e6), transcendentals=0)


def bind(kernel, chunk):
    def bound(*refs):
        kernel(chunk, *refs)

    return bound


def shifted(value, step):
    size = lax.axis_size("zq")
    return lax.ppermute(value, "zq", [(i, (i + step) % size) for i in range(size)])


def turned(value, step):
    size, cols = lax.axis_size(FAR[1]), lax.axis_size("col")
    perm = [
        (i * cols + c, (i + (step if c % 2 == 0 else -step)) % size * cols + c)
        for i in range(size)
        for c in range(cols)
    ]
    return lax.ppermute(value, (*FAR[1], "col"), perm)


def swapped(value, flip):
    return lax.ppermute(value, "col", [(i, i ^ flip) for i in range(lax.axis_size("col"))])


def add(first, second):
    return (first.astype(F32) + second.astype(F32)).astype(BF16)


def body(prepared, sub_off, fac_off, win_col, vis_weights):
    facet_count = fac_off.shape[0]
    strip = prepared[0]
    weights = vis_weights[0]
    facet_len = strip.shape[1]
    grid_len = weights.shape[1]
    col_count = lax.axis_size("col")
    own_rows = facet_len // col_count
    out_cols = LANES * col_count // 2
    place = [lax.axis_index(FAR[0]), lax.axis_index(FAR[1]), lax.axis_index("col")]
    size = lax.axis_size(FAR[1])
    place.append(jnp.where(place[2] % 2 == 0, 1, size - 1))
    place = jnp.stack(place).astype(jnp.int32)
    starts = sub_off.reshape(-1)
    forward_small, backward_small = small_tables()
    grid_forward = grid_table(grid_len, facet_count)
    flips = sorted(range(1, col_count), reverse=True)
    long_rows = pltpu.VMEM((facet_len + XM, LANES), F32)
    grid_rows = pltpu.VMEM((grid_len + XM, LANES), F32)
    planes = [lax.axis_size(axes) for axes in NEAR]
    depths = [lax.axis_size(axes) for axes in FAR]
    blocks = [(p, d, XM, LANES) for p, d in zip(planes, depths)]
    held = [pltpu.VMEM(b, BF16) for b in blocks]
    sems = [pltpu.SemaphoreType.DMA((d,)) for d in depths]

    def contrib(c, strip):
        return call(
            bind(contrib_kernel, c), f"contrib{c}", [blocks[c]], [SMEM, HBM, VMEM],
            [pltpu.VMEM(strip.shape, BF16), long_rows, held[c], pltpu.SemaphoreType.DMA((8,)), sems[c]],
            8, 63, HBM,
        )(starts, strip, forward_small)

    def near(c, value):
        return lax.all_to_all(value, NEAR[c], 0, 0, tiled=True)

    def gather(c, arrived, ks, doubled):
        outs = [(grid_len * (1 + (k in doubled)), LANES) for k in ks]
        made = call(
            lambda *refs: gather_kernel(c, ks, *refs), f"gather{c}{ks[0]}", outs,
            [SMEM, SMEM, HBM], [held[c], grid_rows, sems[c]], 1, 8,
        )(place, fac_off, arrived)
        return dict(zip(ks, made if len(ks) > 1 else [made]))

    def image_of(c, parts):
        return call(
            bind(grid_kernel, c), f"grid{c}", [(grid_len, LANES)], [VMEM] * (2 + len(parts)),
            [], 1.5, 12,
        )(weights, grid_forward, *parts)

    def spread(c, images):
        return call(
            spread_kernel, f"spread{c}", [blocks[1]], [SMEM, SMEM] + [VMEM] * depths[1],
            [grid_rows, held[1], sems[1]], 2, 8, HBM,
        )(place, fac_off, *images)

    def accum(c, returned):
        return call(
            accum_kernel, f"accum{c}", [(own_rows, LANES)] * col_count,
            [SMEM, SMEM, HBM, VMEM], [held[1], long_rows, sems[1]], 5, 14,
        )(place, starts, returned, backward_small)

    def exchange(summed):
        moved = {k: swapped(summed[k], k) for k in flips}
        return [summed[0]] + [moved[k] for k in range(1, col_count)]

    barrier = lax.optimization_barrier
    maps = finish_maps(win_col, out_cols)
    payload0 = contrib(0, strip)
    payload0, strip = barrier((payload0, strip))
    arrived0 = near(0, payload0)
    payload1 = contrib(1, strip)
    arrived0, payload1, maps, grid_forward = barrier((arrived0, payload1, maps, grid_forward))
    arrived1 = near(1, payload1)

    steps = sorted(range(1, depths[0]), key=lambda k: -min(k, depths[0] - k))
    parts0 = gather(0, arrived0, steps, ()) | gather(0, arrived0, [0], ())
    image0 = image_of(0, [parts0[0]] + [shifted(parts0[k], k) for k in steps])

    far, near_side = depths[1] // 2, (depths[1] - 1) // 2
    doubled = [*range(2, far), *range(far + 2, depths[1] - 1)]
    first = [far, far + 1]
    parts1 = gather(1, arrived1, first, ())
    parts1 |= gather(1, arrived1, [k for k in range(depths[1]) if k not in first], doubled)
    ups, downs = barrier(([turned(image0, 1)], [turned(image0, -1)]))
    up = jnp.concatenate([ups[0], parts1[far]])
    down = jnp.concatenate([downs[0], parts1[far + 1]])
    for i in range(far - 1):
        up = turned(up, 1)
        ups.append(up)
        if i < far - 2:
            up = add(up, parts1[far - 1 - i])
    for i in range(near_side - 1):
        down = turned(down, -1)
        downs.append(down)
        if i < near_side - 2:
            down = add(down, parts1[far + 2 + i])
    up = turned(add(up[grid_len:], parts1[1]), 1)
    down = turned(add(down[grid_len:], parts1[depths[1] - 1]), -1)
    images0 = [image0] + ups + downs[::-1]
    image1 = image_of(1, [parts1[0], up, down])
    images0[0], image1 = barrier((image0, image1))
    returned0 = near(1, spread(0, images0))

    ups, downs = [image1], [image1]
    for i in range(far):
        ups.append(turned(ups[-1], 1))
        if i < near_side:
            downs.append(turned(downs[-1], -1))
    spread1 = spread(1, ups + downs[:0:-1])
    returned0, spread1 = barrier((returned0, spread1))
    returned1 = near(1, spread1)
    accum0 = accum(0, returned0)
    strips0 = exchange(accum0)
    strips1 = exchange(accum(1, returned1))

    tile = min(512, own_rows)
    strip_spec = pl.BlockSpec((tile, LANES), lambda i: (i, 0))
    maps_spec = pl.BlockSpec(maps.shape, lambda i: (0, 0, 0, 0))
    wide_spec = pl.BlockSpec((tile, 2 * out_cols), lambda i: (i, 0))
    late = [(1, k) for k in range(2, col_count)]
    early = [(0, k) for k in range(col_count)] + [(1, 0), (1, 1)]
    strips = (strips0, strips1)
    half = pl.pallas_call(
        bind(half_kernel, early),
        name="half",
        grid=(own_rows // tile,),
        out_shape=jax.ShapeDtypeStruct((own_rows, 2 * out_cols), F32),
        in_specs=[SMEM, maps_spec] + [strip_spec] * len(early),
        out_specs=wide_spec,
        compiler_params=pltpu.CompilerParams(vmem_limit_bytes=16 << 20),
        cost_estimate=cost(4),
    )(place, maps, *[strips[c][k] for c, k in early])
    result = pl.pallas_call(
        bind(finish_kernel, late),
        name="finish",
        grid=(own_rows // tile,),
        out_shape=jax.ShapeDtypeStruct((2, own_rows, out_cols), BF16),
        in_specs=[SMEM, maps_spec, wide_spec] + [strip_spec] * len(late),
        out_specs=pl.BlockSpec((2, tile, out_cols), lambda i: (0, i, 0)),
        compiler_params=pltpu.CompilerParams(vmem_limit_bytes=16 << 20),
        cost_estimate=cost(4),
    )(place, maps, half, *[strips[c][k] for c, k in late])
    return result[None]


def solution(mesh):
    facets, cols = mesh.devices.shape
    fine = Mesh(
        mesh.devices.reshape(facets // 16, 2, 2, 4, cols), ("zq", "zp", "xl", "y", "col")
    )
    in_specs = (
        P(FACET, None, None, "col"),
        P(None, "col"),
        P(),
        P(),
        P(FACET, None, None, "col"),
    )
    out_specs = P(FACET, None, "col", None)
    return jax.shard_map(body, mesh=fine, in_specs=in_specs, out_specs=out_specs, check_vma=False)
```
